128 devices in a mesh: ctx: 32 (over y, z, core), head: 4 (over x).
Axes of the slice: x: 4, y: 4, z: 4, core: 2. Of those that a mesh axis runs over, the one named last changes fastest.
Arguments:
- inputs: bfloat16 [8192, 2048], P('ctx'), may hold values from -8 to 8
- key_weight: bfloat16 [2048, 2, 16, 128], P(None, None, 'head'), may hold values from -0.125 to 0.125
- value_weight: bfloat16 [2048, 2, 16, 128], P(None, None, 'head'), may hold values from -0.125 to 0.125
- queries: bfloat16 [8192, 16, 128], P('ctx', 'head'), may hold values from -6 to 6
- betas: float32 [8192, 2, 16], P('ctx', None, 'head'), may hold values from 0.006 to 1.5
- log_decay: float32 [8192, 16], P('ctx', 'head'), may hold values from -1.5 to 0
- grad_out: bfloat16 [8192, 16, 128], P('ctx', 'head'), may hold values from -3 to 3
Outputs:
- key_weight_grad: float32 [2048, 2, 16, 128], P('ctx', None, 'head')
- value_weight_grad: float32 [2048, 2, 16, 128], P('ctx', None, 'head')
- input_grad: bfloat16 [8192, 2048], P('ctx', 'head')
- query_grad: bfloat16 [8192, 16, 128], P('ctx', 'head')
The draws below stay inside these ranges and needn't reach their ends.
All inputs are finite; a program needn't handle non-finite values.
Results may differ from the reference program's by a relative error of at most 0.025.
Values may be sent and summed in bfloat16 or wider, within the bound.
A program may use at most 128 MiB of HBM per device.

```python
import jax
import jax.numpy as jnp
from jax import lax

D = 2048
LAYER_HEADS = 16
HK = 128
REFL = 2
BLOCK = 32
TOK_DEV = 256
SEQUENCE_TOKENS = 8192
N_CTX = 32


def head_modes(key):
    picks = jax.random.randint(jax.random.fold_in(key, 11), (LAYER_HEADS,), 0, 8)
    return picks < 4


def strength_modes(key):
    picks = jax.random.randint(jax.random.fold_in(key, 13), (LAYER_HEADS,), 0, 8)
    return picks < 4


def draw_inputs(key, part):
    random_sources = jax.random.split(jax.random.fold_in(key, 51), 3)
    device_count = SEQUENCE_TOKENS // TOK_DEV
    shared = jax.random.normal(random_sources[0], (device_count, 1, D), jnp.float32)
    pairing = jax.random.permutation(random_sources[1], device_count)
    feature_block = jnp.arange(D) // (D // device_count)
    boost = jnp.where(feature_block[None, :] == pairing[:, None], 4.0, 1.0)
    noise = 0.45 * jax.random.normal(random_sources[2], (device_count, TOK_DEV, D), jnp.float32)
    values = shared + noise * boost[:, None, :]
    values = jnp.clip(values, -8.0, 8.0).reshape(SEQUENCE_TOKENS, D)
    return values.astype(jnp.bfloat16)


def draw_betas(key, part):
    weak = strength_modes(key)
    random_sources = jax.random.split(jax.random.fold_in(key, 37), 2)
    shape = (SEQUENCE_TOKENS, REFL, LAYER_HEADS)
    wide = jnp.exp(jax.random.uniform(random_sources[0], shape, jnp.float32, jnp.log(0.05), jnp.log(1.5)))
    small = jnp.exp(jax.random.uniform(random_sources[1], shape, jnp.float32, jnp.log(0.006), jnp.log(0.0099)))
    return jnp.where(weak[None, None, :], small, wide).astype(jnp.float32)


def draw_log_decay(key, part):
    quick = head_modes(key)
    random_sources = jax.random.split(jax.random.fold_in(key, 23), 6)
    quick_rate = jnp.exp(jax.random.uniform(random_sources[0], (LAYER_HEADS,), jnp.float32, jnp.log(1.0 / 50.0), jnp.log(1.0 / 30.0)))
    slow_rate = 0.4 / SEQUENCE_TOKENS * jnp.exp(jax.random.uniform(random_sources[1], (LAYER_HEADS,), jnp.float32, jnp.log(0.5), jnp.log(2.0)))
    base_rate = jnp.where(quick, quick_rate, slow_rate)
    device_count = SEQUENCE_TOKENS // TOK_DEV
    per_device = jnp.exp(jax.random.uniform(random_sources[2], (device_count, 1, LAYER_HEADS), jnp.float32, jnp.log(0.5), jnp.log(2.0)))
    rough = jax.random.uniform(random_sources[3], (device_count, TOK_DEV, LAYER_HEADS), jnp.float32, 0.5, 1.5)
    event_rates = (base_rate[None, None, :] * per_device * rough).reshape(SEQUENCE_TOKENS, LAYER_HEADS)
    spike_position = jax.random.randint(random_sources[4], (2, LAYER_HEADS), 0, SEQUENCE_TOKENS)
    retained_entries = jax.random.uniform(random_sources[5], (2, LAYER_HEADS), jnp.float32, 0.5, 0.8)
    match_count = jnp.arange(SEQUENCE_TOKENS)[:, None, None] == spike_position[None, :, :]
    spike_events = jnp.sum(jnp.where(match_count, jnp.log(retained_entries)[None, :, :], 0.0), axis=1)
    return (spike_events - event_rates).astype(jnp.float32)


def level_of(key, shape, cuts, low, high):
    loudness, own = 1.0, jax.random.fold_in(key, 6)
    for axis_at, blocks in cuts:
        steps = jnp.exp(jax.random.uniform(jax.random.fold_in(own, axis_at), (blocks,), jnp.float32, low / len(cuts), high / len(cuts)))
        loudness = loudness * jnp.repeat(steps, shape[axis_at] // blocks).reshape([-1 if axis == axis_at else 1 for axis in range(len(shape))])
    return loudness


def bell_draw(stream_key, shape, deviation, limit, shards=(), held_as=jnp.bfloat16):
    factor_of = level_of(stream_key, shape, shards, -0.22, 0.18) if shards else 1.0
    result = jax.random.normal(stream_key, shape, jnp.float32) * deviation * factor_of
    return jnp.minimum(jnp.maximum(result, -limit), limit).astype(held_as)


def setup_inputs(seed: int = 0) -> dict:
    keys = jax.random.split(jax.random.key(seed), 8)
    inputs = draw_inputs(jax.random.fold_in(keys[7], 71), 0)
    key_weight = bell_draw(keys[1], (D, REFL, LAYER_HEADS, HK), D ** -0.5, 0.125, ((2, 4),))
    value_weight = bell_draw(keys[2], (D, REFL, LAYER_HEADS, HK), D ** -0.5, 0.125, ((2, 4),))
    queries = bell_draw(keys[3], (SEQUENCE_TOKENS, LAYER_HEADS, HK), 1.0, 6.0, ((0, 32), (1, 4)))
    betas = draw_betas(jax.random.fold_in(keys[7], 71), 0)
    log_decay = draw_log_decay(jax.random.fold_in(keys[7], 71), 0)
    grad_out = bell_draw(keys[6], (SEQUENCE_TOKENS, LAYER_HEADS, HK), 0.5, 3.0, ((0, 32), (1, 4)))
    return dict(inputs=inputs, key_weight=key_weight, value_weight=value_weight, queries=queries, betas=betas, log_decay=log_decay, grad_out=grad_out)


def block_step(state, key_steps, value_steps, beta_steps, decay_sums, query_rows):
    exact = lax.Precision.HIGHEST
    head_count = key_steps.shape[0]
    step_count = key_steps.shape[1]
    query_count = query_rows.shape[1]
    positions = jnp.arange(step_count)
    strictly = positions[:, None] > positions[None, :]
    gram = jnp.einsum('hik,hpk->hip', key_steps, key_steps, precision=exact)
    gaps = jnp.where(strictly, decay_sums[:, :, None] - decay_sums[:, None, :], 0.0)
    linked = jnp.where(strictly, jnp.exp(gaps), 0.0)
    system = jnp.eye(step_count, dtype=key_steps.dtype) + beta_steps[:, :, None] * gram * linked
    recalled = jnp.einsum('hik,hkw->hiw', key_steps, state, precision=exact)
    target = beta_steps[:, :, None] * (value_steps - jnp.exp(decay_sums)[:, :, None] * recalled)
    writes = jax.scipy.linalg.solve_triangular(system, target, lower=True, unit_diagonal=True)
    final_sum = decay_sums[:, -1:]
    carried = key_steps * jnp.exp(final_sum - decay_sums)[:, :, None]
    state_end = jnp.exp(final_sum)[:, :, None] * state + jnp.einsum('hpk,hpw->hkw', carried, writes, precision=exact)
    token_sums = decay_sums.reshape(head_count, query_count, -1)[:, :, -1]
    slots = jnp.arange(query_count)
    visible = positions[None, :] < (slots[:, None] + 1) * (step_count // query_count)
    fade = jnp.where(visible[None], jnp.exp(jnp.where(visible[None], token_sums[:, :, None] - decay_sums[:, None, :], 0.0)), 0.0)
    reach = jnp.einsum('hsk,hpk->hsp', query_rows, key_steps, precision=exact)
    outputs = jnp.exp(token_sums)[:, :, None] * jnp.einsum('hsk,hkw->hsw', query_rows, state, precision=exact)
    outputs = outputs + jnp.einsum('hsp,hpw->hsw', reach * fade, writes, precision=exact)
    return (state_end, outputs)

def project_inputs(inputs, key_weight, value_weight):
    token_count = inputs.shape[0]
    raw_keys = jnp.dot(inputs.astype(jnp.float32), key_weight.reshape(key_weight.shape[0], -1).astype(jnp.float32), preferred_element_type=jnp.float32)
    raw_keys = raw_keys.reshape((token_count,) + key_weight.shape[1:])
    key_scale = lax.rsqrt(lax.optimization_barrier(jnp.sum(raw_keys * raw_keys, axis=-1, keepdims=True)) + 1e-06)
    key_unit = raw_keys * key_scale
    value_rows = jnp.dot(inputs.astype(jnp.float32), value_weight.reshape(value_weight.shape[0], -1).astype(jnp.float32), preferred_element_type=jnp.float32)
    value_rows = value_rows.astype(jnp.bfloat16).reshape((token_count,) + value_weight.shape[1:])
    return (key_unit.astype(jnp.bfloat16), value_rows, key_unit, key_scale)

def to_substeps(array):
    token_count, refl_count, head_count, width = array.shape
    grouped = array.reshape(token_count // BLOCK, BLOCK, refl_count, head_count, width)
    return grouped.transpose(0, 3, 1, 2, 4).reshape(token_count // BLOCK, head_count, BLOCK * refl_count, width)

def from_substeps(array):
    block_count, head_count, step_count, width = array.shape
    grouped = array.reshape(block_count, head_count, BLOCK, step_count // BLOCK, width)
    return grouped.transpose(0, 2, 3, 1, 4).reshape(block_count * BLOCK, step_count // BLOCK, head_count, width)

def to_blocks(array):
    token_count, head_count, width = array.shape
    return array.reshape(token_count // BLOCK, BLOCK, head_count, width).transpose(0, 2, 1, 3)

def from_blocks(array):
    block_count, head_count, block_len, width = array.shape
    return array.transpose(0, 2, 1, 3).reshape(block_count * block_len, head_count, width)

def arrange(key_rows, value_rows, queries, betas, log_decay, grad_out):
    key_steps = to_substeps(key_rows.astype(jnp.float32))
    value_steps = to_substeps(value_rows.astype(jnp.float32))
    beta_steps = to_substeps(betas[..., None])[..., 0]
    padding = jnp.zeros((log_decay.shape[0], REFL - 1, log_decay.shape[1]), log_decay.dtype)
    decay_steps = to_substeps(jnp.concatenate([log_decay[:, None, :], padding], axis=1)[..., None])[..., 0]
    decay_sums = jnp.cumsum(decay_steps, axis=2)
    query_rows = to_blocks(queries.astype(jnp.float32))
    output_grads = to_blocks(grad_out.astype(jnp.float32))
    return (key_steps, value_steps, beta_steps, decay_sums, query_rows, output_grads)

def key_backward(key_cot, key_unit, key_scale):
    along = lax.optimization_barrier(jnp.sum(key_unit * key_cot, axis=-1, keepdims=True))
    return ((key_cot - key_unit * along) * key_scale).astype(jnp.bfloat16)

def reference(inputs, key_weight, value_weight, queries, betas, log_decay, grad_out):
    key_rows, value_rows, key_unit, key_scale = project_inputs(inputs, key_weight, value_weight)
    key_steps, value_steps, beta_steps, decay_sums, query_rows, output_grads = arrange(key_rows, value_rows, queries, betas, log_decay, grad_out)
    head_count = key_weight.shape[2]
    width = key_weight.shape[3]
    zero_state = jnp.zeros((head_count, width, width), jnp.float32)

    def advance(state, pieces):
        step_keys, step_values, step_betas, step_sums, step_queries = pieces
        end_state, _ = block_step(state, step_keys, step_values, step_betas, step_sums, step_queries)
        return (end_state, state)
    _, block_starts = lax.scan(advance, zero_state, (key_steps, value_steps, beta_steps, decay_sums, query_rows))

    def retreat(adjoint, pieces):
        start_state, step_keys, step_values, step_betas, step_sums, step_queries, step_grads = pieces

        def forward(state_in, keys_in, values_in, queries_in):
            return block_step(state_in, keys_in, values_in, step_betas, step_sums, queries_in)
        _, pullback = jax.vjp(forward, start_state, step_keys, step_values, step_queries)
        previous, key_cot, value_cot, query_cot = pullback((adjoint, step_grads))
        return (previous, (key_cot, value_cot, query_cot))
    _, (key_cots, value_cots, query_cots) = lax.scan(retreat, zero_state, (block_starts, key_steps, value_steps, beta_steps, decay_sums, query_rows, output_grads), reverse=True)
    key_grads = key_backward(from_substeps(key_cots), key_unit, key_scale)
    value_grads = from_substeps(value_cots).astype(jnp.bfloat16)
    token_count = inputs.shape[0]
    stacked = jnp.concatenate([key_grads.reshape(token_count, -1), value_grads.reshape(token_count, -1)], axis=1)
    input_blocks = inputs.reshape(N_CTX, TOK_DEV, -1)
    grad_blocks = stacked.reshape(N_CTX, TOK_DEV, -1)

    def accumulate(totals, pieces):
        term = lax.dot_general(pieces[0].astype(jnp.float32), pieces[1].astype(jnp.float32), (((0,), (0,)), ((), ())), preferred_element_type=jnp.float32)
        rounded = lax.optimization_barrier(term.astype(jnp.bfloat16))
        return (totals + rounded.astype(jnp.float32), None)
    totals, _ = lax.scan(accumulate, jnp.zeros((inputs.shape[1], stacked.shape[1]), jnp.float32), (input_blocks, grad_blocks))
    half_width = totals.shape[1] // 2
    key_weight_grad = totals[:, :half_width].reshape(key_weight.shape)
    value_weight_grad = totals[:, half_width:].reshape(value_weight.shape)
    input_grad = jnp.dot(key_grads.reshape(token_count, -1).astype(jnp.float32), key_weight.reshape(key_weight.shape[0], -1).T.astype(jnp.float32), preferred_element_type=jnp.float32)
    input_grad = input_grad + jnp.dot(value_grads.reshape(token_count, -1).astype(jnp.float32), value_weight.reshape(value_weight.shape[0], -1).T.astype(jnp.float32), preferred_element_type=jnp.float32)
    query_grad = from_blocks(query_cots).astype(jnp.bfloat16)
    return (key_weight_grad, value_weight_grad, input_grad.astype(jnp.bfloat16), query_grad)
```

```python
import functools

import jax
import jax.numpy as jnp
from jax import lax
from jax.experimental import pallas as pl
from jax.experimental.pallas import tpu as pltpu
from jax.sharding import PartitionSpec as P

F32, BF16 = jnp.float32, jnp.bfloat16
T = 256
S = 512
H = 4
N = 128
NB = S // N
TB = N // 2


def dot(a, b, dims, precision=None):
    return lax.dot_general(a, b, (dims, ((), ())), preferred_element_type=F32, precision=precision)


def low(a):
    return a.astype(BF16)


def nn(a, b):
    return dot(low(a), low(b), ((1,), (0,)))


def nt(a, b):
    return dot(low(a), low(b), ((1,), (1,)))


def tn(a, b):
    return dot(low(a), low(b), ((0,), (0,)))


def nn_split(a, b):
    ah, bh = low(a), low(b)
    al, bl = low(a - ah.astype(F32)), low(b - bh.astype(F32))
    d = ((1,), (0,))
    return dot(ah, bh, d) + (dot(ah, bl, d) + dot(al, bh, d))


def iota(shape, axis):
    return lax.broadcasted_iota(jnp.int32, shape, axis)


def inverses(systems):
    row, col = iota((N, N), 0), iota((N, N), 1)
    eye = jnp.where(row == col, 1.0, 0.0)
    near = (row // 8) == (col // 8)
    base = [jnp.where(near, a, 0.0) for a in systems]
    two = [nn_split(a, a) for a in base]
    three = [nn_split(a, b) for a, b in zip(base, two)]
    four = [nn_split(b, b) for b in two]
    head = [eye - a + b - c for a, b, c in zip(base, two, three)]
    inv = [a + nn_split(a, b) for a, b in zip(head, four)]
    size = 8
    while size < N:
        under = ((row // size) == (col // size + 1)) & ((row // (2 * size)) == (col // (2 * size)))
        mid = [nn(jnp.where(under, a, 0.0), t) for a, t in zip(systems, inv)]
        inv = [t - nn(t, m) for t, m in zip(inv, mid)]
        size *= 2
    return inv


def masks():
    row, col = iota((N, N), 0), iota((N, N), 1)
    slot, step = iota((TB, N), 0), iota((TB, N), 1)
    return row > col, step < (slot + 1) * 2


def fade_of(mask, upper, lower):
    return jnp.where(mask, jnp.exp(jnp.where(mask, upper - lower, 0.0)), 0.0)


def prepare_head(h, raw_ref, v_ref, q_ref, do_ref, gcol, grow, bcol, out):
    strict, visible = masks()
    row, col = iota((N, N), 0), iota((N, N), 1)
    eye = jnp.where(row == col, 1.0, 0.0)
    blocks = range(NB)
    ks, gs, bs, systems = [], [], [], []
    for b in blocks:
        rows = pl.ds(b * N, N)
        raw = raw_ref[h, rows, :]
        k = low(raw * lax.rsqrt(jnp.sum(raw * raw, axis=-1, keepdims=True) + 1e-6))
        g, beta = gcol[h, rows, :], bcol[h, rows, :]
        d = fade_of(strict, g, grow[h, :, rows][0:1])
        systems.append(beta * nt(k, k) * d)
        ks.append(k)
        gs.append(g)
        bs.append(beta)
    inv = inverses(systems)
    maps = []
    for b in blocks:
        rows, toks = pl.ds(b * N, N), pl.ds(b * TB, TB)
        k, g, beta = ks[b].astype(F32), gs[b], bs[b]
        v = v_ref[h, rows, :].astype(F32)
        right = jnp.concatenate([low(beta * v), low(beta * jnp.exp(g) * k)], axis=1)
        uy = nn(inv[b], right)
        last = g[N - 1 : N, :]
        kc = low(k * jnp.exp(last - g))
        ends = tn(kc, uy)
        gt = gcol[h, pl.ds(b * N + 1, TB, stride=2), :]
        q, do = q_ref[h, toks, :], do_ref[h, toks, :]
        p = low(nt(q, ks[b]) * fade_of(visible, gt, grow[h, :, rows][0:1]))
        x = jnp.exp(gt) * q.astype(F32) - nn(p, uy[:, N:])
        zy = tn(inv[b], jnp.concatenate([low(tn(p, do)), kc], axis=1))
        a = jnp.exp(last) * eye - ends[:, N:]
        m = (low(a), ends[:, :N], tn(x, do))
        maps.append(m)
        out["u"][h, rows, :] = uy[:, :N]
        out["y"][h, rows, :] = low(uy[:, N:])
        out["z0"][h, rows, :] = zy[:, :N]
        out["yc"][h, rows, :] = low(zy[:, N:])
        out["a"][h, rows, :] = m[0]
        out["b"][h, rows, :] = m[1]
        out["c"][h, rows, :] = m[2]

    def compose(first, second):
        both = nn(second[0], jnp.concatenate([first[0], low(first[1])], axis=1))
        return (
            low(both[:, :N]),
            both[:, N:] + second[1],
            tn(first[0], second[2]) + first[2],
        )

    return compose(compose(maps[0], maps[1]), compose(maps[2], maps[3]))


def column_forms(beta_ref, ld_ref, gcol, grow, bcol):
    exact = lax.Precision.HIGHEST
    step, tok = iota((S, T), 0), iota((S, T), 1)
    running = jnp.where((tok <= step // 2) & (tok // TB == step // N), 1.0, 0.0)
    last = ((1,), (1,))
    ld = ld_ref[...]
    g_col = dot(running, ld, last, exact)
    g_row = dot(ld, running, last, exact)
    b_col = 0.0
    for j in range(2):
        pick = jnp.where((step // 2 == tok) & (step % 2 == j), 1.0, 0.0)
        b_col = b_col + dot(pick, beta_ref[j], last, exact)
    for h in range(H):
        gcol[h] = jnp.broadcast_to(g_col[:, h : h + 1], (S, N))
        bcol[h] = jnp.broadcast_to(b_col[:, h : h + 1], (S, N))
        grow[h] = jnp.broadcast_to(g_row[h : h + 1, :], (8, S))


PRE_OUT = ("u", "y", "z0", "yc", "a", "b", "c")


def first_kernel(
    x_ref, kw_ref, vw_ref, q_in, do_in, beta_ref, ld_ref,
    wre_ref, xt_ref, raw_ref, q_ref, do_ref, gcol, grow, bcol,
    u, y, z0, yc, a, b, c, maps_ref,
    spread, kacc, vacc, v_ref,
):
    i, steps = pl.program_id(0), pl.num_programs(0)
    out = dict(zip(PRE_OUT, (u, y, z0, yc, a, b, c)))
    x = x_ref[...]
    depth = x.shape[1]
    eye = jnp.where(iota((depth, depth), 0) == iota((depth, depth), 1), 1.0, 0.0)
    turned = low(nt(eye, x))
    for m in range(4):
        cy, cz = i // 2, lax.rem(i, 2) * 2 + m // 2
        first, second = (cy, cz) if m % 2 == 0 else (cz, cy)
        xt_ref[m % 2, first, second] = turned[m * 64 : m * 64 + 64]
    for kind, (w_ref, acc) in enumerate(((kw_ref, kacc), (vw_ref, vacc))):
        spread[...] = w_ref[...].astype(F32)
        for pair in range(4):
            cols = []
            for half in range(2):
                rh = 2 * pair + half
                w = low(spread[pl.ds(rh, depth, stride=8), :])
                cols.append(w)
            w = jnp.concatenate(cols, axis=1)
            wre_ref[kind * 4 + pair] = w
            part = dot(x, w, ((1,), (0,)))
            prior = jnp.where(i == 0, 0.0, acc[pair])
            acc[pair] = prior + part

    @pl.when(i == 0)
    def _():
        column_forms(beta_ref, ld_ref, gcol, grow, bcol)
        for source, target in ((q_in, q_ref), (do_in, do_ref)):
            spread[pl.ds(0, 1024), :] = source[...].astype(F32)
            for h in range(H):
                target[h] = low(spread[pl.ds(h, T, stride=4), :])

    @pl.when(i == steps - 1)
    def _():
        for r in range(2):
            for h in range(H):
                rh = r * 4 + h
                lanes = pl.ds((rh % 2) * N, N)
                raw_ref[h, pl.ds(r, T, stride=2), :] = kacc[rh // 2, :, lanes]
                v_ref[h, pl.ds(r, T, stride=2), :] = vacc[rh // 2, :, lanes]

        def head(h, carry):
            total = prepare_head(h, raw_ref, v_round(v_ref), q_ref, do_ref, gcol, grow, bcol, out)
            same = jnp.where(iota((N, N), 0) == iota((N, N), 1), 1.0, 0.0)
            maps_ref[0, h] = jnp.concatenate([total[0], low(total[1])], axis=1)
            maps_ref[1, h] = jnp.concatenate([low(nt(same, total[0])), low(total[2])], axis=1)
            return carry

        lax.fori_loop(0, H, head, 0)


class v_round:
    def __init__(self, ref):
        self.ref = ref

    def __getitem__(self, at):
        return low(self.ref[at])


def full(shape):
    return pl.BlockSpec(shape, lambda i: (0,) * len(shape))


def first_call(x, kw, vw, q, do, beta, ld):
    steps = 8
    depth = 2048 // steps
    sd = jax.ShapeDtypeStruct
    outs = [
        (sd((8, 2048, 256), BF16), pl.BlockSpec((8, depth, 256), lambda i: (0, i, 0))),
    ]
    for shape, kind in (
        [((2, 4, 4, 64, T), BF16), ((H, S, N), F32), ((H, T, N), BF16), ((H, T, N), BF16)]
        + [((H, S, N), F32), ((H, 8, S), F32), ((H, S, N), F32)]
        + [((H, S, N), F32), ((H, S, N), BF16), ((H, S, N), F32), ((H, S, N), BF16)]
        + [((H, S, N), BF16), ((H, S, N), F32), ((H, S, N), F32)]
        + [((2, H, N, 2 * N), BF16)]
    ):
        outs.append((sd(shape, kind), full(shape)))
    return pl.pallas_call(
        first_kernel,
        grid=(steps,),
        in_specs=[
            pl.BlockSpec((T, depth), lambda i: (0, i)),
            pl.BlockSpec((8 * depth, N), lambda i: (i, 0)),
            pl.BlockSpec((8 * depth, N), lambda i: (i, 0)),
            full((1024, N)),
            full((1024, N)),
            full((2, H, T)),
            full((H, T)),
        ],
        out_shape=[o[0] for o in outs],
        out_specs=[o[1] for o in outs],
        scratch_shapes=[
            pltpu.VMEM((8 * depth, N), F32),
            pltpu.VMEM((4, T, 2 * N), F32),
            pltpu.VMEM((4, T, 2 * N), F32),
            pltpu.VMEM((H, S, N), F32),
        ],
        compiler_params=pltpu.CompilerParams(vmem_limit_bytes=60 << 20),
        name="prepare",
    )(x, kw, vw, q, do, beta, ld)


def finish_head(h, start, end, r, dk_out, dv_out, dq_out):
    strict, visible = masks()
    states, ends = [start], [end]
    for b in range(NB - 1):
        rows, back = pl.ds(b * N, N), pl.ds((NB - 1 - b) * N, N)
        states.append(nn(r["a"][h, rows, :], states[-1]) + r["b"][h, rows, :])
        ends.append(tn(r["a"][h, back, :], ends[-1]) + r["c"][h, back, :])
    ends = ends[::-1]
    for b in range(NB):
        rows, toks = pl.ds(b * N, N), pl.ds(b * TB, TB)
        s, ds = low(states[b]), low(ends[b])
        raw = r["raw"][h, rows, :]
        scale = lax.rsqrt(jnp.sum(raw * raw, axis=-1, keepdims=True) + 1e-6)
        unit = raw * scale
        k = low(unit)
        g, beta = r["gcol"][h, rows, :], r["bcol"][h, rows, :]
        g_row = r["grow"][h, :, rows][0:1]
        gt = r["gcol"][h, pl.ds(b * N + 1, TB, stride=2), :]
        q, do = r["q"][h, toks, :], r["do"][h, toks, :]
        w = r["u"][h, rows, :] - nn(r["y"][h, rows, :], s)
        z = r["z0"][h, rows, :] + nn(r["yc"][h, rows, :], ds)
        wl, zl = low(w), low(z)
        dg = low(beta * fade_of(strict, g, g_row) * nt(zl, wl))
        e = low(nt(do, wl) * fade_of(visible, gt, g_row))
        dk = jnp.exp(g[N - 1 : N, :] - g) * nt(wl, ds) - beta * jnp.exp(g) * nt(zl, s)
        dk = dk - nn(dg, k) - tn(dg, k) + tn(e, q)
        dq = jnp.exp(gt) * nt(do, s) + nn(e, k)
        along = jnp.sum(unit * dk, axis=-1, keepdims=True)
        dk_out[h, rows, :] = (dk - unit * along) * scale
        dv_out[h, rows, :] = beta * z
        dq_out[pl.ds(b * TB * H + h, TB, stride=H), :] = dq


SECOND_IN = ("raw", "q", "do", "gcol", "grow", "bcol") + PRE_OUT


def second_kernel(*refs):
    n = len(SECOND_IN)
    r = dict(zip(SECOND_IN, refs[:n]))
    ends_ref, packed_ref, dq_ref, dk, dv, dq = refs[n:]

    def head(h, carry):
        finish_head(h, ends_ref[0, h], ends_ref[1, h], r, dk, dv, dq)
        return carry

    lax.fori_loop(0, H, head, 0)
    for kind, source in enumerate((dk, dv)):
        for j in range(2):
            for h in range(H):
                at = kind * 1024 + (j * 4 + h) * N
                packed_ref[:, at : at + N] = low(source[h, pl.ds(j, T, stride=2), :])
    dq_ref[...] = low(dq[...])


def second_call(values, ends):
    vm = pl.BlockSpec(memory_space=pltpu.VMEM)
    return pl.pallas_call(
        second_kernel,
        in_specs=[vm] * (len(SECOND_IN) + 1),
        out_specs=[vm, vm],
        out_shape=[
            jax.ShapeDtypeStruct((T, 2048), BF16),
            jax.ShapeDtypeStruct((H * T, N), BF16),
        ],
        scratch_shapes=[
            pltpu.VMEM((H, S, N), F32),
            pltpu.VMEM((H, S, N), F32),
            pltpu.VMEM((H * T, N), F32),
        ],
        compiler_params=pltpu.CompilerParams(vmem_limit_bytes=60 << 20),
        name="finish",
    )(*[values[name] for name in SECOND_IN], ends)

MESH = pl.DeviceIdType.MESH


def place():
    me = lax.axis_index("ctx")
    core = lax.rem(me, 2)
    z = lax.rem(me // 2, 4)
    y = me // 8
    return y, z, core


def at(y, z, core):
    return (y * 4 + z) * 2 + core


def around(p, offset):
    return lax.rem(p + offset + 4, 4)


def send(src, dst, send_sem, recv_sem, axis, target):
    return pltpu.make_async_remote_copy(
        src_ref=src, dst_ref=dst, send_sem=send_sem, recv_sem=recv_sem,
        device_id={axis: target}, device_id_type=MESH,
    )


def greet(peers):
    barrier = pltpu.get_barrier_semaphore()
    for axis, target in peers:
        pl.semaphore_signal(barrier, inc=1, device_id={axis: target}, device_id_type=MESH)
    pl.semaphore_wait(barrier, len(peers))


def step_map(second, first):
    both = nn(second[0][:, :N], jnp.concatenate([first[0][:, :N], low(first[1])], axis=1))
    return low(both[:, :N]), both[:, N:] + second[1]


def scan_kernel(maps_ref, out_ref, theirs, chip, zin, yin, states, sin, far, back, sends, recvs):
    y, z, core = place()
    partner = at(y, z, 1 - core)
    zs = [at(y, around(z, o), core) for o in (1, 2, 3)]
    ys = [at(around(y, o), z, core) for o in (1, 2, 3)]
    greet([("ctx", t) for t in [partner] + zs + ys])

    swap = send(maps_ref.at[1 - core], theirs, sends.at[0], recvs.at[0], "ctx", partner)
    swap.start()
    swap.wait()
    for h in range(H):
        mine, other = maps_ref[core, h], theirs[h]
        m = nn(other[:, :N], mine)
        chip[h] = low(jnp.concatenate([m[:, :N], m[:, N:] + other[:, N:].astype(F32)], axis=1))
    zin[0] = chip[z]
    copies = [
        send(chip.at[around(z, o)], zin.at[o], sends.at[o], recvs.at[o], "ctx", zs[o - 1])
        for o in (1, 2, 3)
    ]
    for c in copies:
        c.start()
    for c in copies:
        c.wait()

    def flow(t):
        return jnp.where(core == 0, t, 3 - t)

    held = [zin[lax.rem(z - flow(t) + 4, 4)] for t in range(4)]
    total = held[0]
    for t in range(1, 4):
        m = nn(held[t][:, :N], total)
        total = low(jnp.concatenate([m[:, :N], m[:, N:] + held[t][:, N:].astype(F32)], axis=1))
    yin[0] = total
    copies = [
        send(yin.at[0], yin.at[o], sends.at[3 + o], recvs.at[3 + o], "ctx", ys[o - 1])
        for o in (1, 2, 3)
    ]
    for c in copies:
        c.start()
    for c in copies:
        c.wait()
    state = jnp.zeros((N, N), F32)
    mine = flow(y)
    for t in range(3):
        m = yin[lax.rem(y - flow(t) + 4, 4)]
        new = m[:, N:].astype(F32)
        if t:
            new = new + nn(m[:, :N], state)
        state = jnp.where(t < mine, new, state)
    for t in range(4):
        states[flow(t)] = low(state)
        if t < 3:
            state = nn(held[t][:, :N], state) + held[t][:, N:].astype(F32)
    copies = [
        send(states.at[around(z, o)], sin.at[o], sends.at[6 + o], recvs.at[6 + o], "ctx", zs[o - 1])
        for o in (1, 2, 3)
    ]
    for c in copies:
        c.start()
    sin[0] = states[z]
    for c in copies:
        c.wait()
    for o in range(4):
        h = lax.rem(z - o + 4, 4)
        s = sin[o]
        out_ref[core, h] = s
        m = maps_ref[core, h]
        far[h] = low(nn(m[:, :N], s) + m[:, N:].astype(F32))
    last = send(far, back, sends.at[10], recvs.at[10], "ctx", partner)
    last.start()
    last.wait()
    out_ref[1 - core] = back[...]


def scan_call(maps):
    vm = pl.BlockSpec(memory_space=pltpu.VMEM)
    return pl.pallas_call(
        scan_kernel,
        in_specs=[vm],
        out_specs=vm,
        out_shape=jax.ShapeDtypeStruct((2, H, N, N), BF16),
        scratch_shapes=[
            pltpu.VMEM((H, N, 2 * N), BF16),
            pltpu.VMEM((H, N, 2 * N), BF16),
            pltpu.VMEM((4, N, 2 * N), BF16),
            pltpu.VMEM((4, N, 2 * N), BF16),
            pltpu.VMEM((4, N, N), BF16),
            pltpu.VMEM((4, N, N), BF16),
            pltpu.VMEM((H, N, N), BF16),
            pltpu.VMEM((H, N, N), BF16),
            pltpu.SemaphoreType.DMA((11,)),
            pltpu.SemaphoreType.DMA((11,)),
        ],
        compiler_params=pltpu.CompilerParams(collective_id=0, has_side_effects=True),
        name="scan_maps",
    )(maps)

D = 2048
HALF = 1024
DIRS = (1, -1)


def reduce_kernel(
    packed_ref, xt_ref, wre_hbm, dk_ref, dv_ref, dx_ref,
    packed2, xt2, wre, out1, in1, merge1, own1, out2, in2, merge2, outx, inx, mergex, ownx,
    local, sends, recvs,
):
    y, z, core = place()
    x = lax.axis_index("head")
    partner = at(y, z, 1 - core)
    a, b = jnp.where(core == 0, y, z), jnp.where(core == 0, z, y)

    def along_a(d):
        p = around(a, d)
        return jnp.where(core == 0, at(p, z, core), at(y, p, core))

    def along_b(d):
        p = around(b, d)
        return jnp.where(core == 0, at(y, p, core), at(p, z, core))

    greet(
        [("ctx", partner)]
        + [("ctx", along_a(d)) for d in DIRS]
        + [("ctx", along_b(d)) for d in DIRS]
        + [("head", around(x, d)) for d in DIRS]
    )
    pending = []

    def begin(copy):
        copy.start()
        pending.append(copy)
        return copy

    swap_g = begin(send(packed_ref, packed2, sends.at[0], recvs.at[0], "ctx", partner))
    swap_x = begin(send(xt_ref.at[1 - core], xt2, sends.at[1], recvs.at[1], "ctx", partner))
    fetches = {}
    for n, o in enumerate((2, 1, 3, 0)):
        q = around(x, o)
        rows = pl.ds(pl.multiple_of(q * 512, 512), 512)
        fetches[o] = pltpu.make_async_copy(wre_hbm.at[:, rows, :], wre.at[n], local.at[n])
        fetches[o].start()

    def input_part(n, o):
        fetches[o].wait()
        total = jnp.zeros((T, 512), F32)
        for p in range(8):
            total = total + dot(packed_ref[:, p * 256 : p * 256 + 256], wre[n, p], ((1,), (1,)))
        return total

    hx = T // 2

    def x_copy(kind, i):
        s = 2 + kind * 2 + i
        return send(
            outx.at[kind, i], inx.at[kind, i], sends.at[s], recvs.at[s], "head", around(x, DIRS[i])
        )

    def a_copy(kind, i, r):
        s = 8 + (kind * 2 + i) * 4 + r
        return send(
            out1.at[kind, i, r], in1.at[kind, i, r], sends.at[s], recvs.at[s], "ctx", along_a(DIRS[i])
        )

    def b_copy(kind, i):
        s = 32 + kind * 2 + i
        return send(out2.at[kind, i], in2.at[kind, i], sends.at[s], recvs.at[s], "ctx", along_b(DIRS[i]))

    moves = {}
    far = low(input_part(0, 2))
    for i in range(2):
        outx[0, i] = far[i * hx : (i + 1) * hx]
        moves["x", 0, i] = begin(x_copy(0, i))

    swap_g.wait_recv()
    swap_x.wait_recv()

    def weight_block(o, store):
        q = around(a, o)
        mine = xt_ref[core, q].reshape(256, T)
        theirs = xt2[q].reshape(256, T)

        for side in range(2):

            def columns(n, carry, side=side):
                inner = pl.ds(pl.multiple_of(n * 512, 512), 512)
                cols = pl.ds(pl.multiple_of(n * 512 + side * HALF, 512), 512)
                t = dot(mine, packed_ref[:, cols], ((1,), (0,)))
                t = t + dot(theirs, packed2[:, cols], ((1,), (0,)))
                for bb in range(4):
                    store(lax.rem(bb - b + 4, 4), side, inner, t[bb * 64 : bb * 64 + 64])
                return carry

            lax.fori_loop(0, 2, columns, 0)

    def store_far(r, side, inner, t):
        out1[0, side, r, :, inner] = low(t)

    def store_near(i):
        def store(r, side, inner, t):
            if side == i:
                merge1[i, r, :, inner] = t
            else:
                out1[1, i, r, :, inner] = low(t)

        return store

    def store_own(r, side, inner, t):
        own1[side, r, :, inner] = t

    order = (2, 1, 3, 0)
    weight_block(2, store_far)
    for r in order:
        for i in range(2):
            moves["a", 0, i, r] = begin(a_copy(0, i, r))
    for i in range(2):
        weight_block(DIRS[i], store_near(i))
        for r in order:
            moves["a", 1, i, r] = begin(a_copy(1, i, r))
    for i in range(2):
        near = input_part(1 + i, (1, 3)[i])
        mergex[i] = near[i * hx : (i + 1) * hx]
        outx[1, i] = low(near[(1 - i) * hx : (2 - i) * hx])
        moves["x", 1, i] = begin(x_copy(1, i))
    for i in range(2):
        moves["x", 0, i].wait_recv()
        outx[2, i] = low(mergex[i] + inx[0, i].astype(F32))
        moves["x", 2, i] = begin(x_copy(2, i))
    weight_block(0, store_own)
    ownx[...] = input_part(3, 0)
    for r in order:
        for i in range(2):
            moves["a", 0, i, r].wait_recv()
            out1[2, i, r] = low(merge1[i, r] + in1[0, i, r].astype(F32))
            moves["a", 2, i, r] = begin(a_copy(2, i, r))

    def settle(r, i):
        moves["a", 1, 1 - i, r].wait_recv()
        moves["a", 2, i, r].wait_recv()
        return own1[i, r] + in1[1, 1 - i, r].astype(F32) + in1[2, i, r].astype(F32)

    for i in range(2):
        out2[0, i] = low(settle(2, i))
        moves["b", 0, i] = begin(b_copy(0, i))
    for i, r in enumerate((1, 3)):
        out2[1, i] = low(settle(r, 1 - i))
        moves["b", 1, i] = begin(b_copy(1, i))
        merge2[i] = settle(r, i)
    for i in range(2):
        moves["b", 0, i].wait_recv()
        out2[2, i] = low(merge2[i] + in2[0, i].astype(F32))
        moves["b", 2, i] = begin(b_copy(2, i))
    last = [settle(0, i) for i in range(2)]
    for i in range(2):
        moves["x", 1, 1 - i].wait_recv()
        moves["x", 2, i].wait_recv()
        rows = pl.ds(i * hx, hx)
        dx_ref[rows, :] = low(ownx[rows, :] + inx[1, 1 - i].astype(F32) + inx[2, i].astype(F32))
    for i, out in enumerate((dk_ref, dv_ref)):
        moves["b", 1, 1 - i].wait_recv()
        moves["b", 2, i].wait_recv()
        total = last[i] + in2[1, 1 - i].astype(F32) + in2[2, i].astype(F32)
        for rh in range(8):
            out[pl.ds(rh, 64, stride=8), :] = total[:, rh * N : rh * N + N]
    for copy in pending:
        copy.wait_send()


def reduce_call(packed, xt, wre):
    vm = pl.BlockSpec(memory_space=pltpu.VMEM)
    sd = jax.ShapeDtypeStruct
    return pl.pallas_call(
        reduce_kernel,
        in_specs=[vm, vm, pl.BlockSpec(memory_space=pl.ANY)],
        out_specs=[vm] * 3,
        out_shape=[sd((512, N), F32), sd((512, N), F32), sd((T, 512), BF16)],
        scratch_shapes=[
            pltpu.VMEM((T, D), BF16),
            pltpu.VMEM((4, 4, 64, T), BF16),
            pltpu.VMEM((4, 8, 512, 256), BF16),
            pltpu.VMEM((3, 2, 4, 64, HALF), BF16),
            pltpu.VMEM((3, 2, 4, 64, HALF), BF16),
            pltpu.VMEM((2, 4, 64, HALF), F32),
            pltpu.VMEM((2, 4, 64, HALF), F32),
            pltpu.VMEM((3, 2, 64, HALF), BF16),
            pltpu.VMEM((3, 2, 64, HALF), BF16),
            pltpu.VMEM((2, 64, HALF), F32),
            pltpu.VMEM((3, 2, T // 2, 512), BF16),
            pltpu.VMEM((3, 2, T // 2, 512), BF16),
            pltpu.VMEM((2, T // 2, 512), F32),
            pltpu.VMEM((T, 512), F32),
            pltpu.SemaphoreType.DMA((4,)),
            pltpu.SemaphoreType.DMA((38,)),
            pltpu.SemaphoreType.DMA((38,)),
        ],
        compiler_params=pltpu.CompilerParams(
            collective_id=1, has_side_effects=True, vmem_limit_bytes=60 << 20
        ),
        name="reduce_grads",
    )(packed, xt, wre)


FIRST_OUT = ("wre", "xt", "raw", "q", "do", "gcol", "grow", "bcol") + PRE_OUT + ("maps",)


def shards(inputs, key_weight, value_weight, queries, betas, log_decay, grad_out):
    values = dict(
        zip(
            FIRST_OUT,
            first_call(
                inputs,
                key_weight.reshape(-1, N),
                value_weight.reshape(-1, N),
                queries.reshape(-1, N),
                grad_out.reshape(-1, N),
                betas.transpose(1, 2, 0),
                log_decay.T,
            ),
        )
    )
    ends = scan_call(values["maps"])
    packed, query_grad = second_call(values, ends)
    key_sum, value_sum, input_grad = reduce_call(packed, values["xt"], values["wre"])
    return (
        key_sum.reshape(64, 2, H, N),
        value_sum.reshape(64, 2, H, N),
        input_grad,
        query_grad.reshape(T, H, N),
    )


def solution(mesh):
    in_specs = (
        P("ctx", None),
        P(None, None, "head", None),
        P(None, None, "head", None),
        P("ctx", "head", None),
        P("ctx", None, "head"),
        P("ctx", "head"),
        P("ctx", "head", None),
    )
    out_specs = (
        P("ctx", None, "head", None),
        P("ctx", None, "head", None),
        P("ctx", "head"),
        P("ctx", "head", None),
    )
    return jax.shard_map(shards, mesh=mesh, in_specs=in_specs, out_specs=out_specs, check_vma=False)
```

```python
import functools

import jax
import jax.numpy as jnp
from jax import lax
from jax.experimental import pallas as pl
from jax.experimental.pallas import tpu as pltpu
from jax.sharding import PartitionSpec as P

F32, BF16 = jnp.float32, jnp.bfloat16
T = 256
S = 512
H = 4
N = 128
NB = S // N
TB = N // 2
STEPS = 4
UNIT = 256
GROUP = 4


def dot(a, b, dims, precision=None):
    return lax.dot_general(a, b, (dims, ((), ())), preferred_element_type=F32, precision=precision)


def low(a):
    return a.astype(BF16)


def nn(a, b):
    return dot(low(a), low(b), ((1,), (0,)))


def nt(a, b):
    return dot(low(a), low(b), ((1,), (1,)))


def tn(a, b):
    return dot(low(a), low(b), ((0,), (0,)))


def iota(shape, axis):
    return lax.broadcasted_iota(jnp.int32, shape, axis)


def inverses(systems):
    row, col = iota((N, N), 0), iota((N, N), 1)
    eye = jnp.where(row == col, 1.0, 0.0)
    near = (row // 2) == (col // 2)
    inv = [eye - jnp.where(near, a, 0.0) for a in systems]
    size = 2
    while size < N:
        under = ((row // size) == (col // size + 1)) & ((row // (2 * size)) == (col // (2 * size)))
        mid = [nn(jnp.where(under, a, 0.0), t) for a, t in zip(systems, inv)]
        inv = [t - nn(t, m) for t, m in zip(inv, mid)]
        size *= 2
    return inv


def masks():
    row, col = iota((N, N), 0), iota((N, N), 1)
    slot, step = iota((TB, N), 0), iota((TB, N), 1)
    return row > col, step < (slot + 1) * 2


def fade_of(mask, upper, lower):
    return jnp.where(mask, jnp.exp(jnp.where(mask, upper - lower, 0.0)), 0.0)


def prepare_heads(heads, raw_ref, v_ref, q_ref, do_ref, gcol, grow, bcol, out):
    strict, visible = masks()
    row, col = iota((N, N), 0), iota((N, N), 1)
    eye = jnp.where(row == col, 1.0, 0.0)
    blocks = [(h, b) for h in heads for b in range(NB)]
    ks, systems = [], []
    for h, b in blocks:
        rows = pl.ds(b * N, N)
        raw = raw_ref[h, rows, :]
        k = low(raw * lax.rsqrt(jnp.sum(raw * raw, axis=-1, keepdims=True) + 1e-6))
        d = fade_of(strict, gcol[h, rows, :], grow[h, :, rows][0:1])
        systems.append(bcol[h, rows, :] * nt(k, k) * d)
        ks.append(k)
    inv = [low(t) for t in inverses(systems)]
    pairs, ends, maps = [], [], []
    for n, (h, b) in enumerate(blocks):
        rows = pl.ds(b * N, N)
        beta, g = bcol[h, rows, :], gcol[h, rows, :]
        v = low(v_ref[h, rows, :]).astype(F32)
        right = jnp.concatenate([low(beta * v), low(beta * jnp.exp(g) * ks[n].astype(F32))], axis=1)
        uy = nn(inv[n], right)
        out["u"][h, rows, :] = uy[:, :N]
        pairs.append(low(uy))
        out["y"][h, rows, :] = pairs[n][:, N:]
    kcs = []
    for n, (h, b) in enumerate(blocks):
        g = gcol[h, pl.ds(b * N, N), :]
        kcs.append(low(ks[n].astype(F32) * jnp.exp(g[N - 1 : N, :] - g)))
        ends.append(tn(kcs[n], pairs[n]))
    for n, (h, b) in enumerate(blocks):
        rows, toks = pl.ds(b * N, N), pl.ds(b * TB, TB)
        g = gcol[h, rows, :]
        gt = gcol[h, pl.ds(b * N + 1, TB, stride=2), :]
        q, do = q_ref[h, toks, :], do_ref[h, toks, :]
        p = low(nt(q, ks[n]) * fade_of(visible, gt, grow[h, :, rows][0:1]))
        x = jnp.exp(gt) * q.astype(F32) - nn(p, pairs[n][:, N:])
        out["inv"][h, rows, :], out["kc"][h, rows, :], out["p"][h, toks, :] = inv[n], kcs[n], p
        a = jnp.exp(g[N - 1 : N, :]) * eye - ends[n][:, N:]
        m = (low(a), ends[n][:, :N], tn(x, do))
        maps.append(m)
        out["a"][h, rows, :] = m[0]
        out["b"][h, rows, :] = m[1]
        out["c"][h, rows, :] = m[2]

    def compose(first, second):
        both = nn(second[0], jnp.concatenate([first[0], low(first[1])], axis=1))
        return (
            low(both[:, :N]),
            both[:, N:] + second[1],
            tn(first[0], second[2]) + first[2],
        )

    halves = [compose(maps[n], maps[n + 1]) for n in range(0, len(maps), 2)]
    return [compose(halves[n], halves[n + 1]) for n in range(0, len(halves), 2)]


def late_head(h, r):
    for b in range(NB):
        rows, toks = pl.ds(b * N, N), pl.ds(b * TB, TB)
        right = jnp.concatenate([low(tn(r["p"][h, toks, :], r["do"][h, toks, :])), r["kc"][h, rows, :]], axis=1)
        zy = tn(r["inv"][h, rows, :], right)
        r["z0"][h, rows, :] = zy[:, :N]
        r["yc"][h, rows, :] = low(zy[:, N:])


def pieces(a):
    high = low(a)
    rest = a - high.astype(F32)
    mid = low(rest)
    return high, mid, low(rest - mid.astype(F32))


def column_forms(beta_ref, ld_ref, gcol, grow, bcol):
    step, tok = iota((S, T), 0), iota((S, T), 1)
    running = low(jnp.where((tok <= step // 2) & (tok // TB == step // N), 1.0, 0.0))
    last = ((1,), (1,))
    ld = pieces(ld_ref[...])
    g_col = sum(dot(running, p, last) for p in ld)
    g_row = sum(dot(p, running, last) for p in ld)
    b_col = 0.0
    for j in range(2):
        pick = low(jnp.where((step // 2 == tok) & (step % 2 == j), 1.0, 0.0))
        b_col = b_col + sum(dot(pick, p, last) for p in pieces(beta_ref[j]))
    for h in range(H):
        gcol[h] = jnp.broadcast_to(g_col[:, h : h + 1], (S, N))
        bcol[h] = jnp.broadcast_to(b_col[:, h : h + 1], (S, N))
        grow[h] = jnp.broadcast_to(g_row[h : h + 1, :], (8, S))


MESH = pl.DeviceIdType.MESH


def place():
    me = lax.axis_index("ctx")
    core = lax.rem(me, 2)
    z = lax.rem(me // 2, 4)
    y = me // 8
    return y, z, core


def at(y, z, core):
    return (y * 4 + z) * 2 + core


def around(p, offset):
    return lax.rem(p + offset + 4, 4)


def send(src, dst, send_sem, recv_sem, axis, target):
    return pltpu.make_async_remote_copy(
        src_ref=src, dst_ref=dst, send_sem=send_sem, recv_sem=recv_sem,
        device_id={axis: target}, device_id_type=MESH,
    )


def greet(peers):
    barrier = pltpu.get_barrier_semaphore()
    for axis, target in peers:
        pl.semaphore_signal(barrier, inc=1, device_id={axis: target}, device_id_type=MESH)
    pl.semaphore_wait(barrier, len(peers))


def finish_head(h, start, end, r, dk_out, dv_out, dq_out):
    strict, visible = masks()
    states, ends = [start], [end]
    for b in range(NB - 1):
        rows, back = pl.ds(b * N, N), pl.ds((NB - 1 - b) * N, N)
        states.append(nn(r["a"][h, rows, :], states[-1]) + r["b"][h, rows, :])
        ends.append(tn(r["a"][h, back, :], ends[-1]) + r["c"][h, back, :])
    ends = ends[::-1]
    for b in range(NB):
        rows, toks = pl.ds(b * N, N), pl.ds(b * TB, TB)
        s, ds = low(states[b]), low(ends[b])
        raw = r["raw"][h, rows, :]
        scale = lax.rsqrt(jnp.sum(raw * raw, axis=-1, keepdims=True) + 1e-6)
        unit = raw * scale
        k = low(unit)
        g, beta = r["gcol"][h, rows, :], r["bcol"][h, rows, :]
        g_row = r["grow"][h, :, rows][0:1]
        gt = r["gcol"][h, pl.ds(b * N + 1, TB, stride=2), :]
        q, do = r["q"][h, toks, :], r["do"][h, toks, :]
        w = r["u"][h, rows, :] - nn(r["y"][h, rows, :], s)
        z = r["z0"][h, rows, :] + nn(r["yc"][h, rows, :], ds)
        wl, zl = low(w), low(z)
        dg = low(beta * fade_of(strict, g, g_row) * nt(zl, wl))
        e = low(nt(do, wl) * fade_of(visible, gt, g_row))
        dk = jnp.exp(g[N - 1 : N, :] - g) * nt(wl, ds) - beta * jnp.exp(g) * nt(zl, s)
        dk = dk - nn(dg, k) - tn(dg, k) + tn(e, q)
        dq = jnp.exp(gt) * nt(do, s) + nn(e, k)
        along = jnp.sum(unit * dk, axis=-1, keepdims=True)
        dk_out[rows, :] = (dk - unit * along) * scale
        dv_out[rows, :] = beta * z
        dq_out[pl.ds(b * TB * H + h, TB, stride=H), :] = dq


def scan_phase(r, swap_x, sends, recvs):
    y, z, core = place()
    partner = at(y, z, 1 - core)
    zs = [at(y, around(z, o), core) for o in (1, 2, 3)]
    ys = [at(around(y, o), z, core) for o in (1, 2, 3)]
    maps_ref, out_ref, theirs, chip, zin, yin, states, sin, far, back = (
        r[n] for n in ("maps", "ends", "theirs", "chip", "zin", "yin", "states", "sin", "far", "back")
    )
    swap = send(maps_ref.at[1 - core], theirs, sends.at[0], recvs.at[0], "ctx", partner)
    swap.start()
    late_head(0, r)
    swap.wait()
    swap_x.start()
    for h in range(H):
        mine, other = maps_ref[core, h], theirs[h]
        m = nn(other[:, :N], mine)
        chip[h] = low(jnp.concatenate([m[:, :N], m[:, N:] + other[:, N:].astype(F32)], axis=1))
    zin[0] = chip[z]
    copies = [
        send(chip.at[around(z, o)], zin.at[o], sends.at[o], recvs.at[o], "ctx", zs[o - 1])
        for o in (1, 2, 3)
    ]
    for c in copies:
        c.start()
    late_head(1, r)
    late_head(2, r)
    for c in copies:
        c.wait()

    def flow(t):
        return jnp.where(core == 0, t, 3 - t)

    held = [zin[lax.rem(z - flow(t) + 4, 4)] for t in range(4)]
    total = held[0]
    for t in range(1, 4):
        m = nn(held[t][:, :N], total)
        total = low(jnp.concatenate([m[:, :N], m[:, N:] + held[t][:, N:].astype(F32)], axis=1))
    yin[0] = total
    copies = [
        send(yin.at[0], yin.at[o], sends.at[3 + o], recvs.at[3 + o], "ctx", ys[o - 1])
        for o in (1, 2, 3)
    ]
    for c in copies:
        c.start()
    late_head(3, r)
    for c in copies:
        c.wait()
    state = jnp.zeros((N, N), F32)
    mine = flow(y)
    for t in range(3):
        m = yin[lax.rem(y - flow(t) + 4, 4)]
        new = m[:, N:].astype(F32)
        if t:
            new = new + nn(m[:, :N], state)
        state = jnp.where(t < mine, new, state)
    for t in range(4):
        states[flow(t)] = low(state)
        if t < 3:
            state = nn(held[t][:, :N], state) + held[t][:, N:].astype(F32)
    copies = [
        send(states.at[around(z, o)], sin.at[o], sends.at[6 + o], recvs.at[6 + o], "ctx", zs[o - 1])
        for o in (1, 2, 3)
    ]
    for c in copies:
        c.start()
    sin[0] = states[z]
    for c in copies:
        c.wait()
    for o in range(4):
        h = lax.rem(z - o + 4, 4)
        s = sin[o]
        out_ref[core, h] = s
        m = maps_ref[core, h]
        far[h] = low(nn(m[:, :N], s) + m[:, N:].astype(F32))
    last = send(far, back, sends.at[10], recvs.at[10], "ctx", partner)
    last.start()
    last.wait()
    out_ref[1 - core] = back[...]


D = 2048
HALF = 256
DIRS = (1, -1)


def reduce_phase(r, dk_ref, dv_ref, dx_ref, dq, swap_x, sends, recvs):
    y, z, core = place()
    x = lax.axis_index("head")
    partner = at(y, z, 1 - core)
    a, b = jnp.where(core == 0, y, z), jnp.where(core == 0, z, y)

    def along_a(d):
        p = around(a, d)
        return jnp.where(core == 0, at(p, z, core), at(y, p, core))

    def along_b(d):
        p = around(b, d)
        return jnp.where(core == 0, at(y, p, core), at(p, z, core))

    packed, packed2, xt, xt2 = r["packed"], r["packed2"], r["xt"], r["xt2"]
    out1, in1, merge1, own1 = r["out1"], r["in1"], r["merge1"], r["own1"]
    out2, in2, merge2, own2 = r["out2"], r["in2"], r["merge2"], r["own2"]
    outx, inx, mergex, ownx = r["outx"], r["inx"], r["mergex"], r["ownx"]
    moves, pending = {}, [swap_x]
    hx = T // 2

    def begin(key, copy):
        copy.start()
        pending.append(copy)
        moves[key] = copy

    def x_send(kind, i):
        s = 16 + kind * 2 + i
        begin(
            ("x", kind, i),
            send(outx.at[kind, i], inx.at[kind, i], sends.at[s], recvs.at[s], "head", around(x, DIRS[i])),
        )

    def a_send(kind, i, h):
        s = 22 + (kind * 2 + i) * H + h
        begin(
            ("a", kind, i, h),
            send(out1.at[kind, i, h], in1.at[kind, i, h], sends.at[s], recvs.at[s], "ctx", along_a(DIRS[i])),
        )

    def b_send(kind, i, h):
        s = 46 + (kind * 2 + i) * H + h
        begin(
            ("b", kind, i, h),
            send(out2.at[kind, i, h], in2.at[kind, i, h], sends.at[s], recvs.at[s], "ctx", along_b(DIRS[i])),
        )

    def finish(h):
        finish_head(h, r["ends"][0, h], r["ends"][1, h], r, r["dk"], r["dv"], dq)
        for kind, source in enumerate((r["dk"], r["dv"])):
            for j in range(2):
                lanes = pl.ds((kind * 2 + j) * N, N)
                packed[h, :, lanes] = low(source[pl.ds(j, T, stride=2), :])
        begin(("swap", h), send(packed.at[h], packed2.at[h], sends.at[12 + h], recvs.at[12 + h], "ctx", partner))

    def block(h, o):
        q = around(a, o)
        mine, theirs = xt[core, q].reshape(256, T), xt2[q].reshape(256, T)
        return dot(mine, packed[h], ((1,), (0,))) + dot(theirs, packed2[h], ((1,), (0,)))

    def scatter(t, put):
        for bb in range(4):
            put(lax.rem(bb - b + 4, 4), [t[bb * 64 : bb * 64 + 64, i * HALF : i * HALF + HALF] for i in range(2)])

    def weights(h):
        moves["swap", h].wait_recv()

        def put_far(rel, t):
            for i in range(2):
                out1[0, i, h, rel] = low(t[i])

        scatter(block(h, 2), put_far)
        for i in range(2):
            a_send(0, i, h)
        for i in range(2):

            def put_near(rel, t, i=i):
                merge1[i, h, rel] = t[i]
                out1[1, i, h, rel] = low(t[1 - i])

            scatter(block(h, DIRS[i]), put_near)
            a_send(1, i, h)

        def put_own(rel, t):
            for i in range(2):
                own1[i, h, rel] = t[i]

        scatter(block(h, 0), put_own)

    def pass_a(h):
        for i in range(2):
            moves["a", 0, i, h].wait_recv()
            out1[2, i, h] = low(merge1[i, h] + in1[0, i, h].astype(F32))
            a_send(2, i, h)

    def settle(h):
        for i in range(2):
            moves["a", 1, i, h].wait_recv()
            moves["a", 2, i, h].wait_recv()

        def value(rel, i):
            return own1[i, h, rel] + in1[1, 1 - i, h, rel].astype(F32) + in1[2, i, h, rel].astype(F32)

        for i in range(2):
            out2[0, i, h] = low(value(2, i))
            b_send(0, i, h)
        for i, rel in enumerate((1, 3)):
            out2[1, i, h] = low(value(rel, 1 - i))
            b_send(1, i, h)
            merge2[i, h] = value(rel, i)
        for i in range(2):
            own2[i, h] = value(0, i)

    def pass_b(h):
        for i in range(2):
            moves["b", 0, i, h].wait_recv()
            out2[2, i, h] = low(merge2[i, h] + in2[0, i, h].astype(F32))
            b_send(2, i, h)

    def close(h):
        for i, out in enumerate((dk_ref, dv_ref)):
            moves["b", 1, 1 - i, h].wait_recv()
            moves["b", 2, i, h].wait_recv()
            total = own2[i, h] + in2[1, 1 - i, h].astype(F32) + in2[2, i, h].astype(F32)
            for j in range(2):
                out[pl.ds(j * 4 + h, 64, stride=8), :] = total[:, j * N : j * N + N]

    def input_part(o):
        rows = pl.ds(pl.multiple_of(around(x, o) * 512, 512), 512)
        total = jnp.zeros((T, 512), F32)
        for p in range(8):
            kind, j, m = p // 4, (p % 4) // 2, p % 2
            lanes = pl.ds((kind * 2 + j) * N, N)
            left = jnp.concatenate([packed[2 * m, :, lanes], packed[2 * m + 1, :, lanes]], axis=1)
            total = total + dot(left, r["wre"][p, rows, :], ((1,), (1,)))
        return total

    def input_far():
        far = low(input_part(2))
        for i in range(2):
            outx[0, i] = far[i * hx : (i + 1) * hx]
            x_send(0, i)

    def input_near():
        for i in range(2):
            near = input_part((1, 3)[i])
            mergex[i] = near[i * hx : (i + 1) * hx]
            outx[1, i] = low(near[(1 - i) * hx : (2 - i) * hx])
            x_send(1, i)

    def pass_x():
        for i in range(2):
            moves["x", 0, i].wait_recv()
            outx[2, i] = low(mergex[i] + inx[0, i].astype(F32))
            x_send(2, i)

    def close_x():
        for i in range(2):
            moves["x", 1, 1 - i].wait_recv()
            moves["x", 2, i].wait_recv()
            rows = pl.ds(i * hx, hx)
            dx_ref[rows, :] = low(ownx[rows, :] + inx[1, 1 - i].astype(F32) + inx[2, i].astype(F32))

    finish(0)
    finish(1)
    swap_x.wait_recv()
    weights(0)
    finish(2)
    weights(1)
    pass_a(0)
    finish(3)
    weights(2)
    pass_a(1)
    settle(0)
    weights(3)
    input_far()
    pass_a(2)
    settle(1)
    pass_b(0)
    input_near()
    pass_a(3)
    pass_x()
    settle(2)
    pass_b(1)
    ownx[...] = input_part(0)
    close(0)
    settle(3)
    pass_b(2)
    close(1)
    close_x()
    pass_b(3)
    close(2)
    close(3)
    for copy in pending:
        copy.wait_send()


SCRATCH = dict(
    wre=((8, D, 256), BF16), xt=((2, 4, 4, 64, T), BF16), raw=((H, S, N), F32), v=((H, S, N), F32),
    q=((H, T, N), BF16), do=((H, T, N), BF16), gcol=((H, S, N), F32), grow=((H, 8, S), F32), bcol=((H, S, N), F32),
    u=((H, S, N), F32), y=((H, S, N), BF16), z0=((H, S, N), F32), yc=((H, S, N), BF16),
    a=((H, S, N), BF16), b=((H, S, N), F32), c=((H, S, N), F32),
    inv=((H, S, N), BF16), kc=((H, S, N), BF16), p=((H, T, N), BF16), maps=((2, H, N, 2 * N), BF16),
    spreads=((2, 8 * UNIT, N), F32), kacc=((4, T, 2 * N), F32), vacc=((4, T, 2 * N), F32),
    ends=((2, H, N, N), BF16), theirs=((H, N, 2 * N), BF16), chip=((H, N, 2 * N), BF16),
    zin=((4, N, 2 * N), BF16), yin=((4, N, 2 * N), BF16), states=((4, N, N), BF16), sin=((4, N, N), BF16),
    far=((H, N, N), BF16), back=((H, N, N), BF16),
    dk=((S, N), F32), dv=((S, N), F32), packed=((H, T, 512), BF16), packed2=((H, T, 512), BF16), xt2=((4, 4, 64, T), BF16),
    out1=((3, 2, H, 4, 64, HALF), BF16), in1=((3, 2, H, 4, 64, HALF), BF16),
    merge1=((2, H, 4, 64, HALF), F32), own1=((2, H, 4, 64, HALF), F32),
    out2=((3, 2, H, 64, HALF), BF16), in2=((3, 2, H, 64, HALF), BF16),
    merge2=((2, H, 64, HALF), F32), own2=((2, H, 64, HALF), F32),
    outx=((3, 2, T // 2, 512), BF16), inx=((3, 2, T // 2, 512), BF16), mergex=((2, T // 2, 512), F32), ownx=((T, 512), F32),
    dq=((H * T, N), F32),
)
COPIES = 70


def whole_kernel(x_ref, kw_ref, vw_ref, q_in, do_in, beta_ref, ld_ref, dk_ref, dv_ref, dx_ref, dq_ref, *scratch):
    i, steps = pl.program_id(0), pl.num_programs(0)
    r = dict(zip(SCRATCH, scratch))
    sends, recvs = scratch[len(SCRATCH) :]
    y, z, core = place()
    peers = [("ctx", at(y, z, 1 - core))]
    peers += [("ctx", at(y, around(z, o), core)) for o in (1, 2, 3)]
    peers += [("ctx", at(around(y, o), z, core)) for o in (1, 2, 3)]
    peers += [("head", around(lax.axis_index("head"), d)) for d in DIRS]

    @pl.when(i == 0)
    def _():
        barrier = pltpu.get_barrier_semaphore()
        for axis, target in peers:
            pl.semaphore_signal(barrier, inc=1, device_id={axis: target}, device_id_type=MESH)
        for source, target in ((q_in, r["q"]), (do_in, r["do"])):
            spread = r["spreads"].at[0]
            spread[pl.ds(0, 1024), :] = source[...].astype(F32)
            for h in range(H):
                target[h] = low(spread[pl.ds(h, T, stride=4), :])

    x = x_ref[...]
    depth = x.shape[1]
    eye = low(jnp.where(iota((256, 256), 0) == iota((256, 256), 1), 1.0, 0.0))
    for part in range(depth // 256):
        turned = low(nt(eye, x[:, part * 256 : part * 256 + 256]))
        for m in range(4):
            cz = part * 2 + m // 2
            first, second = (i, cz) if m % 2 == 0 else (cz, i)
            r["xt"][m % 2, first, second] = turned[m * 64 : m * 64 + 64]
    units = [(kind, part) for part in range(depth // UNIT) for kind in range(2)]
    weights, accs = (kw_ref, vw_ref), (r["kacc"], r["vacc"])
    spreads = r["spreads"]

    def open_unit(n):
        kind, part = units[n]
        spreads[n % 2] = weights[kind][pl.ds(part * UNIT * 8, UNIT * 8), :].astype(F32)

    def use_unit(n):
        kind, part = units[n]
        inner = pl.ds(part * UNIT, UNIT)
        for pair in range(4):
            cols = [
                low(spreads[n % 2, pl.ds(2 * pair + half, UNIT, stride=8), :]) for half in range(2)
            ]
            w = jnp.concatenate(cols, axis=1)
            r["wre"][kind * 4 + pair, pl.ds(pl.multiple_of(i * depth + part * UNIT, UNIT), UNIT), :] = w
            product = dot(x[:, part * UNIT : part * UNIT + UNIT], w, ((1,), (0,)))
            if part == 0:
                prior = jnp.where(i == 0, 0.0, accs[kind][pair])
            else:
                prior = accs[kind][pair]
            accs[kind][pair] = prior + product

    open_unit(0)
    for n in range(len(units)):
        if n + 1 < len(units):
            open_unit(n + 1)
        use_unit(n)

    @pl.when(i == steps - 1)
    def _():
        pl.semaphore_wait(pltpu.get_barrier_semaphore(), len(peers))
        column_forms(beta_ref, ld_ref, r["gcol"], r["grow"], r["bcol"])
        for j in range(2):
            for h in range(H):
                rh = j * 4 + h
                lanes = pl.ds((rh % 2) * N, N)
                r["raw"][h, pl.ds(j, T, stride=2), :] = r["kacc"][rh // 2, :, lanes]
                r["v"][h, pl.ds(j, T, stride=2), :] = r["vacc"][rh // 2, :, lanes]
        same = low(jnp.where(iota((N, N), 0) == iota((N, N), 1), 1.0, 0.0))
        totals = prepare_heads(range(H), r["raw"], r["v"], r["q"], r["do"], r["gcol"], r["grow"], r["bcol"], r)
        for h, total in enumerate(totals):
            r["maps"][0, h] = jnp.concatenate([total[0], low(total[1])], axis=1)
            r["maps"][1, h] = jnp.concatenate([low(nt(same, total[0])), low(total[2])], axis=1)
        swap_x = send(
            r["xt"].at[1 - core], r["xt2"], sends.at[11], recvs.at[11], "ctx", at(y, z, 1 - core)
        )
        scan_phase(r, swap_x, sends, recvs)
        reduce_phase(r, dk_ref, dv_ref, dx_ref, r["dq"], swap_x, sends, recvs)
        dq_ref[...] = low(r["dq"][...])


def full(shape):
    return pl.BlockSpec(shape, lambda i: (0,) * len(shape))


def whole_call(x, kw, vw, q, do, beta, ld):
    depth = D // STEPS
    sd = jax.ShapeDtypeStruct
    outs = [((512, N), F32), ((512, N), F32), ((T, 512), BF16), ((H * T, N), BF16)]
    return pl.pallas_call(
        whole_kernel,
        grid=(STEPS,),
        in_specs=[
            pl.BlockSpec((T, depth), lambda i: (0, i)),
            pl.BlockSpec((8 * depth, N), lambda i: (i, 0)),
            pl.BlockSpec((8 * depth, N), lambda i: (i, 0)),
            full((H * T, N)),
            full((H * T, N)),
            full((2, H, T)),
            full((H, T)),
        ],
        out_shape=[sd(*o) for o in outs],
        out_specs=[full(o[0]) for o in outs],
        scratch_shapes=[pltpu.VMEM(*v) for v in SCRATCH.values()]
        + [pltpu.SemaphoreType.DMA((COPIES,))] * 2,
        compiler_params=pltpu.CompilerParams(
            collective_id=0, has_side_effects=True, vmem_limit_bytes=63 << 20
        ),
        name="whole",
    )(x, kw, vw, q, do, beta, ld)


def hand_over(*refs):
    half = len(refs) // 2
    for source, target in zip(refs[:half], refs[half:]):
        target[...] = source[...]


def shards(inputs, key_weight, value_weight, queries, betas, log_decay, grad_out):
    results = whole_call(
        inputs,
        key_weight.reshape(-1, N),
        value_weight.reshape(-1, N),
        queries.reshape(-1, N),
        grad_out.reshape(-1, N),
        betas.transpose(1, 2, 0),
        log_decay.T,
    )
    vm = pl.BlockSpec(memory_space=pltpu.VMEM)
    key_sum, value_sum, input_grad, query_grad = pl.pallas_call(
        hand_over,
        in_specs=[vm] * 4,
        out_specs=[vm] * 4,
        out_shape=[jax.ShapeDtypeStruct(v.shape, v.dtype) for v in results],
        name="hand_over",
    )(*results)
    return (
        key_sum.reshape(64, 2, H, N),
        value_sum.reshape(64, 2, H, N),
        input_grad,
        query_grad.reshape(T, H, N),
    )


def solution(mesh):
    in_specs = (
        P("ctx", None),
        P(None, None, "head", None),
        P(None, None, "head", None),
        P("ctx", "head", None),
        P("ctx", None, "head"),
        P("ctx", "head"),
        P("ctx", "head", None),
    )
    out_specs = (
        P("ctx", None, "head", None),
        P("ctx", None, "head", None),
        P("ctx", "head"),
        P("ctx", "head", None),
    )
    return jax.shard_map(shards, mesh=mesh, in_specs=in_specs, out_specs=out_specs, check_vma=False)
```

```python
import functools

import jax
import jax.numpy as jnp
from jax import lax
from jax.experimental import pallas as pl
from jax.experimental.pallas import tpu as pltpu
from jax.sharding import PartitionSpec as P

F32, BF16 = jnp.float32, jnp.bfloat16
T = 256
S = 512
H = 4
N = 128
NB = S // N
TB = N // 2
STEPS = 4
UNIT = 256
GROUP = 4


def dot(a, b, dims, precision=None):
    return lax.dot_general(a, b, (dims, ((), ())), preferred_element_type=F32, precision=precision)


def low(a):
    return a.astype(BF16)


def nn(a, b):
    return dot(low(a), low(b), ((1,), (0,)))


def nt(a, b):
    return dot(low(a), low(b), ((1,), (1,)))


def tn(a, b):
    return dot(low(a), low(b), ((0,), (0,)))


def iota(shape, axis):
    return lax.broadcasted_iota(jnp.int32, shape, axis)


def inverses(systems):
    row, col = iota((N, N), 0), iota((N, N), 1)
    eye = jnp.where(row == col, 1.0, 0.0)
    near = (row // 2) == (col // 2)
    inv = [eye - jnp.where(near, a, 0.0) for a in systems]
    size = 2
    while size < N:
        under = ((row // size) == (col // size + 1)) & ((row // (2 * size)) == (col // (2 * size)))
        mid = [nn(jnp.where(under, a, 0.0), t) for a, t in zip(systems, inv)]
        inv = [t - nn(t, m) for t, m in zip(inv, mid)]
        size *= 2
    return inv


def masks():
    row, col = iota((N, N), 0), iota((N, N), 1)
    slot, step = iota((TB, N), 0), iota((TB, N), 1)
    return row > col, step < (slot + 1) * 2


def fade_of(mask, upper, lower):
    return jnp.where(mask, jnp.exp(jnp.where(mask, upper - lower, 0.0)), 0.0)


def prepare_heads(heads, raw_ref, v_ref, q_ref, do_ref, gcol, grow, bcol, out):
    strict, visible = masks()
    row, col = iota((N, N), 0), iota((N, N), 1)
    eye = jnp.where(row == col, 1.0, 0.0)
    blocks = [(h, b) for h in heads for b in range(NB)]
    ks, systems = [], []
    for h, b in blocks:
        rows = pl.ds(b * N, N)
        raw = raw_ref[h, rows, :]
        k = low(raw * lax.rsqrt(jnp.sum(raw * raw, axis=-1, keepdims=True) + 1e-6))
        d = bcol[h, rows, :] * fade_of(strict, gcol[h, rows, :], grow[h, :, rows][0:1])
        out["bd"][h, rows, :] = d
        systems.append(nt(k, k) * d)
        ks.append(k)
    inv = [low(t) for t in inverses(systems)]
    pairs, ends, maps = [], [], []
    for n, (h, b) in enumerate(blocks):
        rows = pl.ds(b * N, N)
        beta, g = bcol[h, rows, :], gcol[h, rows, :]
        v = low(v_ref[h, rows, :]).astype(F32)
        grown = beta * jnp.exp(g)
        out["be"][h, rows, :] = grown
        right = jnp.concatenate([low(beta * v), low(grown * ks[n].astype(F32))], axis=1)
        uy = nn(inv[n], right)
        out["u"][h, rows, :] = uy[:, :N]
        pairs.append(low(uy))
        out["y"][h, rows, :] = pairs[n][:, N:]
    kcs = []
    for n, (h, b) in enumerate(blocks):
        g = gcol[h, pl.ds(b * N, N), :]
        rest = jnp.exp(g[N - 1 : N, :] - g)
        out["rest"][h, pl.ds(b * N, N), :] = rest
        kcs.append(low(ks[n].astype(F32) * rest))
        ends.append(tn(kcs[n], pairs[n]))
    for n, (h, b) in enumerate(blocks):
        rows, toks = pl.ds(b * N, N), pl.ds(b * TB, TB)
        g = gcol[h, rows, :]
        gt = gcol[h, pl.ds(b * N + 1, TB, stride=2), :]
        q, do = q_ref[h, toks, :], do_ref[h, toks, :]
        fade = fade_of(visible, gt, grow[h, :, rows][0:1])
        out["fade"][h, toks, :] = fade
        p = low(nt(q, ks[n]) * fade)
        x = jnp.exp(gt) * q.astype(F32) - nn(p, pairs[n][:, N:])
        out["inv"][h, rows, :], out["kc"][h, rows, :], out["p"][h, toks, :] = inv[n], kcs[n], p
        a = jnp.exp(g[N - 1 : N, :]) * eye - ends[n][:, N:]
        m = (low(a), ends[n][:, :N], tn(x, do))
        maps.append(m)
        out["a"][h, rows, :] = m[0]
        out["b"][h, rows, :] = m[1]
        out["c"][h, rows, :] = m[2]

    def compose(first, second):
        both = nn(second[0], jnp.concatenate([first[0], low(first[1])], axis=1))
        return (
            low(both[:, :N]),
            both[:, N:] + second[1],
            tn(first[0], second[2]) + first[2],
        )

    halves = [compose(maps[n], maps[n + 1]) for n in range(0, len(maps), 2)]
    return [compose(halves[n], halves[n + 1]) for n in range(0, len(halves), 2)]


def late_head(h, r):
    for b in range(NB):
        rows, toks = pl.ds(b * N, N), pl.ds(b * TB, TB)
        right = jnp.concatenate([low(tn(r["p"][h, toks, :], r["do"][h, toks, :])), r["kc"][h, rows, :]], axis=1)
        zy = tn(r["inv"][h, rows, :], right)
        r["z0"][h, rows, :] = zy[:, :N]
        r["yc"][h, rows, :] = low(zy[:, N:])


def pieces(a):
    high = low(a)
    rest = a - high.astype(F32)
    mid = low(rest)
    return high, mid, low(rest - mid.astype(F32))


def column_forms(beta_ref, ld_ref, gcol, grow, bcol):
    step, tok = iota((S, T), 0), iota((S, T), 1)
    running = low(jnp.where((tok <= step // 2) & (tok // TB == step // N), 1.0, 0.0))
    last = ((1,), (1,))
    ld = pieces(ld_ref[...])
    g_col = sum(dot(running, p, last) for p in ld)
    g_row = sum(dot(p, running, last) for p in ld)
    b_col = 0.0
    for j in range(2):
        pick = low(jnp.where((step // 2 == tok) & (step % 2 == j), 1.0, 0.0))
        b_col = b_col + sum(dot(pick, p, last) for p in pieces(beta_ref[j]))
    for h in range(H):
        gcol[h] = jnp.broadcast_to(g_col[:, h : h + 1], (S, N))
        bcol[h] = jnp.broadcast_to(b_col[:, h : h + 1], (S, N))
        grow[h] = jnp.broadcast_to(g_row[h : h + 1, :], (8, S))


MESH = pl.DeviceIdType.MESH


def place():
    me = lax.axis_index("ctx")
    core = lax.rem(me, 2)
    z = lax.rem(me // 2, 4)
    y = me // 8
    return y, z, core


def at(y, z, core):
    return (y * 4 + z) * 2 + core


def around(p, offset):
    return lax.rem(p + offset + 4, 4)


def send(src, dst, send_sem, recv_sem, axis, target):
    return pltpu.make_async_remote_copy(
        src_ref=src, dst_ref=dst, send_sem=send_sem, recv_sem=recv_sem,
        device_id={axis: target}, device_id_type=MESH,
    )


def greet(peers):
    barrier = pltpu.get_barrier_semaphore()
    for axis, target in peers:
        pl.semaphore_signal(barrier, inc=1, device_id={axis: target}, device_id_type=MESH)
    pl.semaphore_wait(barrier, len(peers))


def finish_heads(heads, r, dk_out, dv_out, dq_out):
    states, ends = {}, {}
    for h in heads:
        states[h, 0], ends[h, NB - 1] = r["ends"][0, h], r["ends"][1, h]
    for b in range(NB - 1):
        for h in heads:
            rows, back = pl.ds(b * N, N), pl.ds((NB - 1 - b) * N, N)
            states[h, b + 1] = low(nn(r["a"][h, rows, :], states[h, b]) + r["b"][h, rows, :])
            ends[h, NB - 2 - b] = low(tn(r["a"][h, back, :], ends[h, NB - 1 - b]) + r["c"][h, back, :])
    blocks = [(h, b) for b in range(NB) for h in heads]
    ws, zs = {}, {}
    for h, b in blocks:
        rows = pl.ds(b * N, N)
        ws[h, b] = low(r["u"][h, rows, :] - nn(r["y"][h, rows, :], states[h, b]))
        z = r["z0"][h, rows, :] + nn(r["yc"][h, rows, :], ends[h, b])
        dv_out[h, rows, :] = r["bcol"][h, rows, :] * z
        zs[h, b] = low(z)
    for h, b in blocks:
        rows, toks = pl.ds(b * N, N), pl.ds(b * TB, TB)
        s, ds, wl, zl = states[h, b], ends[h, b], ws[h, b], zs[h, b]
        raw = r["raw"][h, rows, :]
        scale = lax.rsqrt(jnp.sum(raw * raw, axis=-1, keepdims=True) + 1e-6)
        unit = raw * scale
        k = low(unit)
        gt = r["gcol"][h, pl.ds(b * N + 1, TB, stride=2), :]
        q, do = r["q"][h, toks, :], r["do"][h, toks, :]
        dg = low(r["bd"][h, rows, :] * nt(zl, wl))
        e = low(nt(do, wl) * r["fade"][h, toks, :])
        dk = r["rest"][h, rows, :] * nt(wl, ds) - r["be"][h, rows, :] * nt(zl, s)
        dk = dk - nn(dg, k) - tn(dg, k) + tn(e, q)
        dq = jnp.exp(gt) * nt(do, s) + nn(e, k)
        along = jnp.sum(unit * dk, axis=-1, keepdims=True)
        dk_out[h, rows, :] = (dk - unit * along) * scale
        dq_out[pl.ds(b * TB * H + h, TB, stride=H), :] = dq


FAR_FIRST = (1, 0, 2)


def scan_phase(r, swap_x, sends, recvs):
    y, z, core = place()
    partner = at(y, z, 1 - core)
    zs = [at(y, around(z, o), core) for o in (1, 2, 3)]
    ys = [at(around(y, o), z, core) for o in (1, 2, 3)]
    maps_ref, out_ref, theirs, chip, zin, yin, states, sin, far, back = (
        r[n] for n in ("maps", "ends", "theirs", "chip", "zin", "yin", "states", "sin", "far", "back")
    )
    swap = send(maps_ref.at[1 - core], theirs, sends.at[0], recvs.at[0], "ctx", partner)
    swap.start()
    late_head(0, r)
    swap.wait()
    swap_x.start()
    for h in range(H):
        mine, other = maps_ref[core, h], theirs[h]
        m = nn(other[:, :N], mine)
        chip[h] = low(jnp.concatenate([m[:, :N], m[:, N:] + other[:, N:].astype(F32)], axis=1))
    zin[0] = chip[z]
    copies = [
        send(chip.at[around(z, o)], zin.at[o], sends.at[o], recvs.at[o], "ctx", zs[o - 1])
        for o in (1, 2, 3)
    ]
    for n in FAR_FIRST:
        copies[n].start()
    late_head(1, r)
    late_head(2, r)
    for c in copies:
        c.wait()

    def flow(t):
        return jnp.where(core == 0, t, 3 - t)

    held = [zin[lax.rem(z - flow(t) + 4, 4)] for t in range(4)]
    total = held[0]
    for t in range(1, 4):
        m = nn(held[t][:, :N], total)
        total = low(jnp.concatenate([m[:, :N], m[:, N:] + held[t][:, N:].astype(F32)], axis=1))
    yin[0] = total
    copies = [
        send(yin.at[0], yin.at[o], sends.at[3 + o], recvs.at[3 + o], "ctx", ys[o - 1])
        for o in (1, 2, 3)
    ]
    gives = [jnp.logical_xor(y + o < 4, core == 1) for o in (1, 2, 3)]
    takes = [jnp.logical_xor(y >= o, core == 1) for o in (1, 2, 3)]
    for n in FAR_FIRST:
        pl.when(gives[n])(copies[n].start)
    late_head(3, r)
    for c, give, take in zip(copies, gives, takes):
        pl.when(take)(c.wait_recv)
        pl.when(give)(c.wait_send)
    state = jnp.zeros((N, N), F32)
    mine = flow(y)
    for t in range(3):
        m = yin[lax.rem(y - flow(t) + 4, 4)]
        new = m[:, N:].astype(F32)
        if t:
            new = new + nn(m[:, :N], state)
        state = jnp.where(t < mine, new, state)
    for t in range(4):
        states[flow(t)] = low(state)
        if t < 3:
            state = nn(held[t][:, :N], state) + held[t][:, N:].astype(F32)
    copies = [
        send(states.at[around(z, o)], sin.at[o], sends.at[6 + o], recvs.at[6 + o], "ctx", zs[o - 1])
        for o in (1, 2, 3)
    ]
    for n in FAR_FIRST:
        copies[n].start()
    sin[0] = states[z]
    for c in copies:
        c.wait()
    for o in range(4):
        h = lax.rem(z - o + 4, 4)
        s = sin[o]
        out_ref[core, h] = s
        m = maps_ref[core, h]
        far[h] = low(nn(m[:, :N], s) + m[:, N:].astype(F32))
    last = send(far, back, sends.at[10], recvs.at[10], "ctx", partner)
    last.start()
    last.wait()
    out_ref[1 - core] = back[...]


D = 2048
HALF = 256
DIRS = (1, -1)


PARTS = {None: (0, 4), 0: (0, 1), 1: (1, 2), 2: (3, 1)}


def reduce_phase(r, dk_ref, dv_ref, dx_ref, dq, swap_x, sends, recvs):
    y, z, core = place()
    x = lax.axis_index("head")
    partner = at(y, z, 1 - core)
    a, b = jnp.where(core == 0, y, z), jnp.where(core == 0, z, y)

    def along_a(d):
        p = around(a, d)
        return jnp.where(core == 0, at(p, z, core), at(y, p, core))

    def along_b(d):
        p = around(b, d)
        return jnp.where(core == 0, at(y, p, core), at(p, z, core))

    packed, packed2, xt, xt2 = r["packed"], r["packed2"], r["xt"], r["xt2"]
    out1, in1, merge1, own1 = r["out1"], r["in1"], r["merge1"], r["own1"]
    out2, in2, merge2, own2 = r["out2"], r["in2"], r["merge2"], r["own2"]
    outx, inx, mergex, ownx = r["outx"], r["inx"], r["mergex"], r["ownx"]
    moves, pending = {}, [swap_x]
    hx = T // 2

    def begin(key, copy):
        copy.start()
        pending.append(copy)
        moves[key] = copy

    def x_send(kind, i):
        s = 16 + kind * 2 + i
        begin(
            ("x", kind, i),
            send(outx.at[kind, i], inx.at[kind, i], sends.at[s], recvs.at[s], "head", around(x, DIRS[i])),
        )

    def a_send(kind, i, h, part):
        rows = pl.ds(*PARTS[part])
        s = 22 + ((kind * 2 + i) * H + h if part is None else 48 + (kind * 2 + i) * 3 + part)
        begin(
            ("a", kind, i, h, part),
            send(
                out1.at[kind, i, h, rows], in1.at[kind, i, h, rows],
                sends.at[s], recvs.at[s], "ctx", along_a(DIRS[i]),
            ),
        )

    def b_send(kind, i, h):
        s = 46 + (kind * 2 + i) * H + h
        begin(
            ("b", kind, i, h),
            send(out2.at[kind, i, h], in2.at[kind, i, h], sends.at[s], recvs.at[s], "ctx", along_b(DIRS[i])),
        )

    def finish(*heads):
        finish_heads(heads, r, r["dk"], r["dv"], dq)
        for h in heads:
            hand_in(h)

    def hand_in(h):
        for kind, source in enumerate((r["dk"], r["dv"])):
            for j in range(2):
                lanes = pl.ds((kind * 2 + j) * N, N)
                packed[h, :, lanes] = low(source[h, pl.ds(j, T, stride=2), :])
        begin(("swap", h), send(packed.at[h], packed2.at[h], sends.at[12 + h], recvs.at[12 + h], "ctx", partner))

    def block(h, o):
        q = around(a, o)
        mine, theirs = xt[core, q].reshape(256, T), xt2[q].reshape(256, T)
        return dot(mine, packed[h], ((1,), (0,))) + dot(theirs, packed2[h], ((1,), (0,)))

    def scatter(t, put):
        for bb in range(4):
            rel = lax.rem(bb - b + 4, 4)
            slot = jnp.where(rel == 2, 0, jnp.where(rel == 0, 3, (rel + 1) // 2))
            put(slot, [t[bb * 64 : bb * 64 + 64, i * HALF : i * HALF + HALF] for i in range(2)])

    def weights(h):
        moves["swap", h].wait_recv()

        def put_far(rel, t):
            for i in range(2):
                out1[0, i, h, rel] = low(t[i])

        parts = parts_of(h)
        scatter(block(h, 2), put_far)
        for i in range(2):
            a_send(0, i, h, parts[0])
        for i in range(2):

            def put_near(rel, t, i=i):
                merge1[i, h, rel] = t[i]
                out1[1, i, h, rel] = low(t[1 - i])

            scatter(block(h, DIRS[i]), put_near)
        for n, part in enumerate(parts):
            for i in range(2):
                if n:
                    a_send(0, i, h, part)
                a_send(1, i, h, part)

        def put_own(rel, t):
            for i in range(2):
                own1[i, h, rel] = t[i]

        scatter(block(h, 0), put_own)

    def parts_of(h):
        return (0, 1, 2) if h == H - 1 else (None,)

    def pass_a(h, part=None):
        first, count = PARTS[part]
        rows = pl.ds(first, count)
        for i in range(2):
            moves["a", 0, i, h, part].wait_recv()
            out1[2, i, h, rows] = low(merge1[i, h, rows] + in1[0, i, h, rows].astype(F32))
            a_send(2, i, h, part)

    def settle(h, part=None):
        for i in range(2):
            moves["a", 1, i, h, part].wait_recv()
            moves["a", 2, i, h, part].wait_recv()

        def value(slot, i):
            return own1[i, h, slot] + in1[1, 1 - i, h, slot].astype(F32) + in1[2, i, h, slot].astype(F32)

        if part in (None, 0):
            for i in range(2):
                out2[0, i, h] = low(value(0, i))
                b_send(0, i, h)
        if part in (None, 1):
            for i in range(2):
                out2[1, i, h] = low(value(1 + i, 1 - i))
                b_send(1, i, h)
                merge2[i, h] = value(1 + i, i)
        if part in (None, 2):
            for i in range(2):
                own2[i, h] = value(3, i)

    def pass_b(h):
        for i in range(2):
            moves["b", 0, i, h].wait_recv()
            out2[2, i, h] = low(merge2[i, h] + in2[0, i, h].astype(F32))
            b_send(2, i, h)

    def close(h):
        for i, out in enumerate((dk_ref, dv_ref)):
            moves["b", 1, 1 - i, h].wait_recv()
            moves["b", 2, i, h].wait_recv()
            total = own2[i, h] + in2[1, 1 - i, h].astype(F32) + in2[2, i, h].astype(F32)
            for j in range(2):
                out[pl.ds(j * 4 + h, 64, stride=8), :] = total[:, j * N : j * N + N]

    def input_part(o):
        rows = pl.ds(pl.multiple_of(around(x, o) * 512, 512), 512)
        total = jnp.zeros((T, 512), F32)
        for p in range(8):
            kind, j, m = p // 4, (p % 4) // 2, p % 2
            lanes = pl.ds((kind * 2 + j) * N, N)
            left = jnp.concatenate([packed[2 * m, :, lanes], packed[2 * m + 1, :, lanes]], axis=1)
            total = total + dot(left, r["wre"][p, rows, :], ((1,), (1,)))
        return total

    def input_far():
        far = low(input_part(2))
        for i in range(2):
            outx[0, i] = far[i * hx : (i + 1) * hx]
            x_send(0, i)

    def input_near():
        for i in range(2):
            near = input_part((1, 3)[i])
            mergex[i] = near[i * hx : (i + 1) * hx]
            outx[1, i] = low(near[(1 - i) * hx : (2 - i) * hx])
            x_send(1, i)

    def pass_x():
        for i in range(2):
            moves["x", 0, i].wait_recv()
            outx[2, i] = low(mergex[i] + inx[0, i].astype(F32))
            x_send(2, i)

    def close_x():
        for i in range(2):
            moves["x", 1, 1 - i].wait_recv()
            moves["x", 2, i].wait_recv()
            rows = pl.ds(i * hx, hx)
            dx_ref[rows, :] = low(ownx[rows, :] + inx[1, 1 - i].astype(F32) + inx[2, i].astype(F32))

    finish(0)
    finish(1)
    swap_x.wait_recv()
    weights(0)
    weights(1)
    finish(2)
    pass_a(0)
    finish(3)
    pass_a(1)
    weights(2)
    weights(3)
    input_far()
    settle(0)
    pass_a(2)
    pass_b(0)
    settle(1)
    pass_a(3, 0)
    input_near()
    pass_a(3, 1)
    pass_a(3, 2)
    pass_x()
    pass_b(1)
    settle(2)
    ownx[...] = input_part(0)
    close(0)
    settle(3, 0)
    pass_b(2)
    settle(3, 1)
    close(1)
    close_x()
    pass_b(3)
    close(2)
    settle(3, 2)
    close(3)
    for copy in pending:
        copy.wait_send()


SCRATCH = dict(
    wre=((8, D, 256), BF16), xt=((2, 4, 4, 64, T), BF16), raw=((H, S, N), F32), v=((H, S, N), F32),
    q=((H, T, N), BF16), do=((H, T, N), BF16), gcol=((H, S, N), F32), grow=((H, 8, S), F32), bcol=((H, S, N), F32),
    u=((H, S, N), F32), y=((H, S, N), BF16), z0=((H, S, N), F32), yc=((H, S, N), BF16),
    a=((H, S, N), BF16), b=((H, S, N), F32), c=((H, S, N), F32),
    inv=((H, S, N), BF16), kc=((H, S, N), BF16), p=((H, T, N), BF16), maps=((2, H, N, 2 * N), BF16),
    spreads=((2, 8 * UNIT, N), F32), kacc=((4, T, 2 * N), F32), vacc=((4, T, 2 * N), F32),
    ends=((2, H, N, N), BF16), theirs=((H, N, 2 * N), BF16), chip=((H, N, 2 * N), BF16),
    zin=((4, N, 2 * N), BF16), yin=((4, N, 2 * N), BF16), states=((4, N, N), BF16), sin=((4, N, N), BF16),
    far=((H, N, N), BF16), back=((H, N, N), BF16),
    dk=((H, S, N), F32), dv=((H, S, N), F32),
    bd=((H, S, N), F32), be=((H, S, N), F32), rest=((H, S, N), F32), fade=((H, T, N), F32), packed=((H, T, 512), BF16), packed2=((H, T, 512), BF16), xt2=((4, 4, 64, T), BF16),
    out1=((3, 2, H, 4, 64, HALF), BF16), in1=((3, 2, H, 4, 64, HALF), BF16),
    merge1=((2, H, 4, 64, HALF), F32), own1=((2, H, 4, 64, HALF), F32),
    out2=((3, 2, H, 64, HALF), BF16), in2=((3, 2, H, 64, HALF), BF16),
    merge2=((2, H, 64, HALF), F32), own2=((2, H, 64, HALF), F32),
    outx=((3, 2, T // 2, 512), BF16), inx=((3, 2, T // 2, 512), BF16), mergex=((2, T // 2, 512), F32), ownx=((T, 512), F32),
    dq=((H * T, N), F32),
)
COPIES = 88


def whole_kernel(x_ref, kw_ref, vw_ref, q_in, do_in, beta_ref, ld_ref, dk_ref, dv_ref, dx_ref, dq_ref, *scratch):
    i, steps = pl.program_id(0), pl.num_programs(0)
    r = dict(zip(SCRATCH, scratch))
    sends, recvs = scratch[len(SCRATCH) :]
    y, z, core = place()
    peers = [("ctx", at(y, z, 1 - core))]
    peers += [("ctx", at(y, around(z, o), core)) for o in (1, 2, 3)]
    peers += [("ctx", at(around(y, o), z, core)) for o in (1, 2, 3)]
    peers += [("head", around(lax.axis_index("head"), d)) for d in DIRS]

    @pl.when(i == 0)
    def _():
        r["yin"][...] = jnp.zeros_like(r["yin"])
        barrier = pltpu.get_barrier_semaphore()
        for axis, target in peers:
            pl.semaphore_signal(barrier, inc=1, device_id={axis: target}, device_id_type=MESH)
        for source, target in ((q_in, r["q"]), (do_in, r["do"])):
            spread = r["spreads"].at[0]
            spread[pl.ds(0, 1024), :] = source[...].astype(F32)
            for h in range(H):
                target[h] = low(spread[pl.ds(h, T, stride=4), :])

    x = x_ref[...]
    depth = x.shape[1]
    eye = low(jnp.where(iota((256, 256), 0) == iota((256, 256), 1), 1.0, 0.0))
    for part in range(depth // 256):
        turned = low(nt(eye, x[:, part * 256 : part * 256 + 256]))
        for m in range(4):
            cz = part * 2 + m // 2
            first, second = (i, cz) if m % 2 == 0 else (cz, i)
            r["xt"][m % 2, first, second] = turned[m * 64 : m * 64 + 64]
    units = [(kind, part) for part in range(depth // UNIT) for kind in range(2)]
    weights, accs = (kw_ref, vw_ref), (r["kacc"], r["vacc"])
    spreads = r["spreads"]

    def open_unit(n):
        kind, part = units[n]
        spreads[n % 2] = weights[kind][pl.ds(part * UNIT * 8, UNIT * 8), :].astype(F32)

    def use_unit(n):
        kind, part = units[n]
        inner = pl.ds(part * UNIT, UNIT)
        for pair in range(4):
            cols = [
                low(spreads[n % 2, pl.ds(2 * pair + half, UNIT, stride=8), :]) for half in range(2)
            ]
            w = jnp.concatenate(cols, axis=1)
            r["wre"][kind * 4 + pair, pl.ds(pl.multiple_of(i * depth + part * UNIT, UNIT), UNIT), :] = w
            product = dot(x[:, part * UNIT : part * UNIT + UNIT], w, ((1,), (0,)))
            if part == 0:
                prior = jnp.where(i == 0, 0.0, accs[kind][pair])
            else:
                prior = accs[kind][pair]
            accs[kind][pair] = prior + product

    open_unit(0)
    for n in range(len(units)):
        if n + 1 < len(units):
            open_unit(n + 1)
        use_unit(n)

    @pl.when(i == steps - 1)
    def _():
        pl.semaphore_wait(pltpu.get_barrier_semaphore(), len(peers))
        column_forms(beta_ref, ld_ref, r["gcol"], r["grow"], r["bcol"])
        for j in range(2):
            for h in range(H):
                rh = j * 4 + h
                lanes = pl.ds((rh % 2) * N, N)
                r["raw"][h, pl.ds(j, T, stride=2), :] = r["kacc"][rh // 2, :, lanes]
                r["v"][h, pl.ds(j, T, stride=2), :] = r["vacc"][rh // 2, :, lanes]
        same = low(jnp.where(iota((N, N), 0) == iota((N, N), 1), 1.0, 0.0))
        totals = prepare_heads(range(H), r["raw"], r["v"], r["q"], r["do"], r["gcol"], r["grow"], r["bcol"], r)
        for h, total in enumerate(totals):
            r["maps"][0, h] = jnp.concatenate([total[0], low(total[1])], axis=1)
            r["maps"][1, h] = jnp.concatenate([low(nt(same, total[0])), low(total[2])], axis=1)
        swap_x = send(
            r["xt"].at[1 - core], r["xt2"], sends.at[11], recvs.at[11], "ctx", at(y, z, 1 - core)
        )
        scan_phase(r, swap_x, sends, recvs)
        reduce_phase(r, dk_ref, dv_ref, dx_ref, r["dq"], swap_x, sends, recvs)
        dq_ref[...] = low(r["dq"][...])


def full(shape):
    return pl.BlockSpec(shape, lambda i: (0,) * len(shape))


def whole_call(x, kw, vw, q, do, beta, ld):
    depth = D // STEPS
    sd = jax.ShapeDtypeStruct
    outs = [((512, N), F32), ((512, N), F32), ((T, 512), BF16), ((H * T, N), BF16)]
    return pl.pallas_call(
        whole_kernel,
        grid=(STEPS,),
        in_specs=[
            pl.BlockSpec((T, depth), lambda i: (0, i)),
            pl.BlockSpec((8 * depth, N), lambda i: (i, 0)),
            pl.BlockSpec((8 * depth, N), lambda i: (i, 0)),
            full((H * T, N)),
            full((H * T, N)),
            full((2, H, T)),
            full((H, T)),
        ],
        out_shape=[sd(*o) for o in outs],
        out_specs=[full(o[0]) for o in outs],
        scratch_shapes=[pltpu.VMEM(*v) for v in SCRATCH.values()]
        + [pltpu.SemaphoreType.DMA((COPIES,))] * 2,
        compiler_params=pltpu.CompilerParams(
            collective_id=0, has_side_effects=True, vmem_limit_bytes=63 << 20
        ),
        name="whole",
    )(x, kw, vw, q, do, beta, ld)


def hand_over(*refs):
    half = len(refs) // 2
    for source, target in zip(refs[:half], refs[half:]):
        target[...] = source[...]


def shards(inputs, key_weight, value_weight, queries, betas, log_decay, grad_out):
    results = whole_call(
        inputs,
        key_weight.reshape(-1, N),
        value_weight.reshape(-1, N),
        queries.reshape(-1, N),
        grad_out.reshape(-1, N),
        betas.transpose(1, 2, 0),
        log_decay.T,
    )
    vm = pl.BlockSpec(memory_space=pltpu.VMEM)
    key_sum, value_sum, input_grad, query_grad = pl.pallas_call(
        hand_over,
        in_specs=[vm] * 4,
        out_specs=[vm] * 4,
        out_shape=[jax.ShapeDtypeStruct(v.shape, v.dtype) for v in results],
        name="hand_over",
    )(*results)
    return (
        key_sum.reshape(64, 2, H, N),
        value_sum.reshape(64, 2, H, N),
        input_grad,
        query_grad.reshape(T, H, N),
    )


def solution(mesh):
    in_specs = (
        P("ctx", None),
        P(None, None, "head", None),
        P(None, None, "head", None),
        P("ctx", "head", None),
        P("ctx", None, "head"),
        P("ctx", "head"),
        P("ctx", "head", None),
    )
    out_specs = (
        P("ctx", None, "head", None),
        P("ctx", None, "head", None),
        P("ctx", "head"),
        P("ctx", "head", None),
    )
    return jax.shard_map(shards, mesh=mesh, in_specs=in_specs, out_specs=out_specs, check_vma=False)
```
